256 devices in a mesh: layer: 32 (over y, z_hi, core), dp: 8 (over x, z_lo).
Axes of the slice: x: 4, y: 4, z: 8 (z_hi: 4, z_lo: 2; z = z_hi * 2 + z_lo), core: 2. Of those that a mesh axis runs over, the one named last changes fastest.
Arguments:
- c_guess: float32 [32, 1024, 512], P('layer', 'dp'), may hold values from -6 to 6
- adj_guess: float32 [32, 1024, 512], P('layer', 'dp'), may hold values from -6 to 6
- norm_gain: float32 [64, 512], P('layer'), may hold values from 0.5 to 1.5
- w_up: bfloat16 [64, 512, 2048], P('layer'), may hold values from -0.25 to 0.25
- w_down: bfloat16 [64, 2048, 512], P('layer'), may hold values from -0.125 to 0.125
- coarse_rate: float32 [32, 512], P('layer'), may hold values from 0.5 to 1
Outputs:
- c_points: float32 [32, 1024, 512], P('layer', 'dp')
- adj_points: float32 [32, 1024, 512], P('layer', 'dp')
- grad_up: float32 [64, 512, 2048], P('layer', 'dp')
- grad_down: float32 [64, 2048, 512], P('layer', 'dp')
The draws below stay inside these ranges and needn't reach their ends.
All inputs are finite; a program needn't handle non-finite values.
Results may differ from the reference program's by a relative error of at most 0.018.
Values may be sent and summed in bfloat16 or wider, within the bound.
No kernel may reach another device: no remote copies, remote signals or barrier semaphores. Data moves between devices by JAX's collectives and lax.ppermute only.
A program may use at most 64 MiB of HBM per device.

```python
import jax
import jax.numpy as jnp
from jax import lax

MODEL_WIDTH = 512
FF = 2048
LPB = 2
DEPTH = 64
TOKENS = 1024
N_LAYER = 32


def draw_coarse_rate(key, part):
    root_random_key = jax.random.fold_in(key, 4711)
    gentle_rate_key, quick_rate_key, selection_key, spike_rows_key, spike_size_key = jax.random.split(root_random_key, 5)
    fraction = jax.random.uniform(gentle_rate_key, (N_LAYER, MODEL_WIDTH), jnp.float32, 0.0, 1.0)
    slow_rates = jnp.exp(jnp.log(jnp.float32(0.1)) / N_LAYER * fraction)
    fast_rates = jnp.exp(jax.random.uniform(quick_rate_key, (N_LAYER, MODEL_WIDTH), jnp.float32, jnp.log(0.5), jnp.log(0.9)))
    slow_channel = jax.random.randint(selection_key, (1, MODEL_WIDTH), 0, 2)
    rate_values = jnp.where(slow_channel == 1, slow_rates, fast_rates)
    spike_row_count = jax.random.randint(spike_rows_key, (2,), 0, N_LAYER)
    block_number = jnp.arange(N_LAYER, dtype=jnp.int32)
    spike_selected = jnp.any(block_number[:, None] == spike_row_count[None, :], axis=1)
    spike_multiplier = jax.random.uniform(spike_size_key, (N_LAYER, MODEL_WIDTH), jnp.float32, 0.55, 0.8)
    rate_values = jnp.where(spike_selected[:, None], jnp.maximum(rate_values * spike_multiplier, 0.5), rate_values)
    return jnp.clip(rate_values, 0.5, 1.0).astype(jnp.float32)


def levels(own_key, shape, shards, least, top_value):
    gain, own = 1.0, jax.random.fold_in(own_key, 6)
    for axis_at, shards_of in shards:
        steps = jnp.exp(jax.random.uniform(jax.random.fold_in(own, axis_at), (shards_of,), jnp.float32, least / len(shards), top_value / len(shards)))
        gain = gain * jnp.repeat(steps, shape[axis_at] // shards_of).reshape([-1 if axis == axis_at else 1 for axis in range(len(shape))])
    return gain


def normal_values(rng, shape, spread, reach, shards=(), held_as=jnp.bfloat16):
    loudness = levels(rng, shape, shards, -0.22, 0.18) if shards else 1.0
    entries = jax.random.normal(rng, shape, jnp.float32) * spread * loudness
    return jnp.minimum(jnp.maximum(entries, -reach), reach).astype(held_as)


def setup_inputs(seed: int = 0) -> dict:
    key_list = jax.random.split(jax.random.key(seed), 7)
    return {
        "c_guess": normal_values(key_list[0], (N_LAYER, TOKENS, MODEL_WIDTH), 1.0, 6.0, ((0, 32), (1, 8)), jnp.float32),
        "adj_guess": normal_values(key_list[1], (N_LAYER, TOKENS, MODEL_WIDTH), 1.0, 6.0, ((0, 32), (1, 8)), jnp.float32),
        "norm_gain": jnp.clip(1.0 + 0.1 * jax.random.normal(key_list[2], (DEPTH, MODEL_WIDTH), jnp.float32), 0.5, 1.5),
        "w_up": normal_values(key_list[3], (DEPTH, MODEL_WIDTH, FF), MODEL_WIDTH ** -0.5, 0.25, ((0, 32),)),
        "w_down": normal_values(key_list[4], (DEPTH, FF, MODEL_WIDTH), FF ** -0.5, 0.125, ((0, 32),)),
        "coarse_rate": draw_coarse_rate(jax.random.fold_in(key_list[6], 71), 0),
    }


eps = 1e-06
step_length = 0.5

def normalize(state):
    inverse_rms = lax.rsqrt(lax.optimization_barrier(jnp.mean(state * state, axis=-1, keepdims=True)) + eps)
    return (state * inverse_rms, inverse_rms)

def layer_forward(state, gain_row, up_matrix, down_matrix):
    unit_state, inverse_rms = normalize(state)
    normed = (unit_state * gain_row).astype(jnp.bfloat16)
    preact = jnp.dot(normed, up_matrix, preferred_element_type=jnp.float32)
    hidden = jax.nn.silu(preact).astype(jnp.bfloat16)
    return state + step_length * jnp.dot(hidden, down_matrix, preferred_element_type=jnp.float32)

def layer_backward(state, cotangent, gain_row, up_matrix, down_matrix):
    unit_state, inverse_rms = normalize(state)
    normed = (unit_state * gain_row).astype(jnp.bfloat16)
    preact = jnp.dot(normed, up_matrix, preferred_element_type=jnp.float32)
    hidden = jax.nn.silu(preact).astype(jnp.bfloat16)
    sigmoid_pre = jax.nn.sigmoid(preact)
    out_grad = (step_length * cotangent).astype(jnp.bfloat16)
    hidden_grad = jnp.dot(out_grad, down_matrix.T, preferred_element_type=jnp.float32)
    pre_grad = (hidden_grad * sigmoid_pre * (1.0 + preact * (1.0 - sigmoid_pre))).astype(jnp.bfloat16)
    normed_grad = jnp.dot(pre_grad, up_matrix.T, preferred_element_type=jnp.float32)
    unit_grad = normed_grad * gain_row
    inner = lax.optimization_barrier(jnp.mean(unit_grad * unit_state, axis=-1, keepdims=True))
    new_cotangent = cotangent + inverse_rms * (unit_grad - unit_state * inner)
    return (new_cotangent, normed, pre_grad, hidden, out_grad)

def block_forward(state, gains, ups, downs):
    for depth_index in range(gains.shape[0]):
        state = layer_forward(state, gains[depth_index], ups[depth_index], downs[depth_index])
    return state

def block_inputs(state, gains, ups, downs):
    inputs = [state]
    for depth_index in range(gains.shape[0] - 1):
        state = layer_forward(state, gains[depth_index], ups[depth_index], downs[depth_index])
        inputs.append(state)
    return inputs

def block_backward(inputs, cotangent, gains, ups, downs):
    normed_list, pre_list, hidden_list, out_list = ([], [], [], [])
    for depth_index in reversed(range(gains.shape[0])):
        cotangent, normed, pre_grad, hidden, out_grad = layer_backward(inputs[depth_index], cotangent, gains[depth_index], ups[depth_index], downs[depth_index])
        normed_list.insert(0, normed)
        pre_list.insert(0, pre_grad)
        hidden_list.insert(0, hidden)
        out_list.insert(0, out_grad)
    factors = (jnp.stack(normed_list), jnp.stack(pre_list), jnp.stack(hidden_list), jnp.stack(out_list))
    return (cotangent, factors)

def reference(c_guess, adj_guess, norm_gain, w_up, w_down, coarse_rate):
    gains = norm_gain.reshape(N_LAYER, LPB, MODEL_WIDTH)
    ups = w_up.reshape(N_LAYER, LPB, MODEL_WIDTH, FF)
    downs = w_down.reshape(N_LAYER, LPB, FF, MODEL_WIDTH)

    def relax_forward(items):
        return block_forward(items[0], items[1], items[2], items[3])
    ends = lax.map(relax_forward, (c_guess, gains, ups, downs))

    def forward_step(carry, items):
        block_end, decay, guess = items
        updated = block_end + decay * (carry - guess)
        return (updated, updated)
    _, later_points = lax.scan(forward_step, c_guess[0], (ends[:-1], coarse_rate[:-1], c_guess[:-1]))
    c_points = jnp.concatenate([c_guess[:1], later_points], axis=0)

    def relax_adjoint(items):
        point, cotangent, gain_blk, up_blk, down_blk = items
        inputs = block_inputs(point, gain_blk, up_blk, down_blk)
        begin, _ = block_backward(inputs, cotangent, gain_blk, up_blk, down_blk)
        return begin
    starts = lax.map(relax_adjoint, (c_points, adj_guess, gains, ups, downs))

    def adjoint_step(carry, items):
        begin, decay, guess = items
        updated = begin + decay * (carry - guess)
        return (updated, updated)
    _, earlier_points = lax.scan(adjoint_step, adj_guess[-1], (starts[1:], coarse_rate[1:], adj_guess[1:]), reverse=True)
    adj_points = jnp.concatenate([earlier_points, adj_guess[-1:]], axis=0)

    def gradients(items):
        point, cotangent, gain_blk, up_blk, down_blk = items
        inputs = block_inputs(point, gain_blk, up_blk, down_blk)
        _, factors = block_backward(inputs, cotangent, gain_blk, up_blk, down_blk)
        normed, pre_grad, hidden, out_grad = factors
        up_grad = jnp.einsum('ltd,ltf->ldf', normed.astype(jnp.float32), pre_grad.astype(jnp.float32))
        down_grad = jnp.einsum('ltf,ltd->lfd', hidden.astype(jnp.float32), out_grad.astype(jnp.float32))
        return (up_grad, down_grad)
    up_grads, down_grads = lax.map(gradients, (c_points, adj_points, gains, ups, downs))
    return (c_points, adj_points, up_grads.reshape(DEPTH, MODEL_WIDTH, FF), down_grads.reshape(DEPTH, FF, MODEL_WIDTH))
```

```python
import jax
import jax.numpy as jnp
from jax import lax
from jax.sharding import Mesh
from jax.sharding import PartitionSpec as P

LAYER = ("y", "zh", "c")
DP = ("x", "zl")

eps = 1e-06
step_length = 0.5
f32 = jnp.float32
bf16 = jnp.bfloat16


def dot(a, b):
    return jnp.dot(a, b, preferred_element_type=f32)


def dot_t(a, b):
    return lax.dot_general(a, b, (((1,), (1,)), ((), ())), preferred_element_type=f32)


def dot_tokens(a, b):
    return lax.dot_general(a, b, (((0,), (0,)), ((), ())), preferred_element_type=f32)


def normalize(state):
    inverse_rms = lax.rsqrt(jnp.mean(state * state, axis=-1, keepdims=True) + eps)
    return state * inverse_rms, inverse_rms


def silu_parts(preact):
    s = 0.5 + 0.5 * jnp.tanh(0.5 * preact)
    return (preact * s).astype(bf16), s * (1.0 + preact * (1.0 - s))


def layer_forward(state, gain, up, down):
    unit, _ = normalize(state)
    normed = (unit * gain).astype(bf16)
    hidden, _ = silu_parts(dot(normed, up))
    return state + step_length * dot(hidden, down)


def input_cotangent(cotangent, normed_grad, unit, inverse_rms, gain):
    unit_grad = normed_grad * gain
    inner = jnp.mean(unit_grad * unit, axis=-1, keepdims=True)
    return cotangent + inverse_rms * (unit_grad - unit * inner)


def forward_states(point, gains, ups, downs):
    unit0, inv0 = normalize(point)
    normed0 = (unit0 * gains[0]).astype(bf16)
    hidden0, slope0 = silu_parts(dot(normed0, ups[0]))
    state = point + step_length * dot(hidden0, downs[0])
    unit1, inv1 = normalize(state)
    normed1 = (unit1 * gains[1]).astype(bf16)
    hidden1, slope1 = silu_parts(dot(normed1, ups[1]))
    return (unit0, inv0, normed0, hidden0, slope0), (unit1, inv1, normed1, hidden1, slope1)


def shift_pairs(size, k):
    return [(i, (i + k) % size) for i in range(size)]


def split_rows(a):
    hi = a.astype(bf16)
    lo = (a - hi.astype(f32)).astype(bf16)
    return hi, lo


def exchange_cores(x):
    return lax.ppermute(x, "c", [(0, 1), (1, 0)])


def line_exchange(payload, axis):
    return [lax.ppermute(payload, axis, shift_pairs(4, k)) for k in (1, 2, 3)]


def pack(rate, shift):
    hi, lo = split_rows(rate)
    pad = jnp.zeros((14, rate.shape[-1]), bf16)
    return jnp.concatenate([shift.astype(bf16), hi, lo, pad], 0)


def unpack(payload, rows):
    shift = payload[:rows].astype(f32)
    rate = payload[rows : rows + 1].astype(f32) + payload[rows + 1 : rows + 2].astype(f32)
    return rate, shift


def fold(pieces, carry, rate, mask, order):
    for k in order:
        a, b = pieces[k - 1]
        keep = mask(k)
        carry = jnp.where(keep, a * carry + b, carry)
        rate = jnp.where(keep, a * rate, rate)
    return rate, carry


def forward_sweep(decay, shift):
    c = lax.axis_index("c")
    zh = lax.axis_index("zh")
    y = lax.axis_index("y")
    half = shift.shape[0] // 2
    first = c == 0
    width = shift.shape[1]
    low, high = shift[:half], shift[half:]
    mine = jnp.where(first, low, high)
    give = jnp.concatenate(
        [jnp.where(first, high, low), jnp.broadcast_to(decay[None], (8, width))], 0
    )
    got = exchange_cores(give)
    other, other_rate = got[:half], got[half : half + 1]
    rate0 = jnp.where(first, decay[None], other_rate)
    rate1 = jnp.where(first, other_rate, decay[None])
    b0 = jnp.where(first, mine, other)
    b1 = jnp.where(first, other, mine)
    pair = (rate0 * rate1, rate1 * b0 + b1)
    pieces_z = [unpack(p, half) for p in line_exchange(pack(*pair), "zh")]
    one = jnp.ones_like(rate0)
    zero = jnp.zeros_like(b0)
    before_rate, before = fold(pieces_z, zero, one, lambda k: zh >= k, (3, 2, 1))
    row = (pair[0] * before_rate, pair[0] * before + pair[1])
    row = fold(pieces_z, row[1], row[0], lambda k: zh < k, (3, 2, 1))
    pieces_y = [unpack(p, half) for p in line_exchange(pack(*row), "y")]
    _, rows_before = fold(pieces_y, zero, one, lambda k: y >= k, (3, 2, 1))
    entry = before_rate * rows_before + before
    later = rate0 * entry + b0
    got = exchange_cores(jnp.where(first, later, entry))
    own = jnp.where(first, entry, later)
    point = jnp.concatenate([jnp.where(first, own, got), jnp.where(first, got, own)], 0)
    rates = (rate0, rate1, [p[0] for p in pieces_z], [p[0] for p in pieces_y])
    return point, rates


def backward_sweep(rates, shift):
    rate0, rate1, rates_z, rates_y = rates
    c = lax.axis_index("c")
    zh = lax.axis_index("zh")
    y = lax.axis_index("y")
    half = shift.shape[0] // 2
    first = c == 0
    low, high = shift[:half], shift[half:]
    mine = jnp.where(first, low, high)
    other = exchange_cores(jnp.where(first, high, low))
    b0 = jnp.where(first, mine, other)
    b1 = jnp.where(first, other, mine)
    pair_rate, pair = rate0 * rate1, rate0 * b1 + b0
    got = line_exchange(pair.astype(bf16), "zh")
    pieces_z = [(a, p.astype(f32)) for a, p in zip(rates_z, got)]
    one = jnp.ones_like(rate0)
    zero = jnp.zeros_like(b0)
    after_rate, after = fold(pieces_z, zero, one, lambda k: zh < k, (1, 2, 3))
    _, row = fold(pieces_z, pair_rate * after + pair, one, lambda k: zh >= k, (1, 2, 3))
    got = line_exchange(row.astype(bf16), "y")
    pieces_y = [(a, p.astype(f32)) for a, p in zip(rates_y, got)]
    _, rows_after = fold(pieces_y, zero, one, lambda k: y < k, (1, 2, 3))
    entry = after_rate * rows_after + after
    earlier = rate1 * entry + b1
    got = exchange_cores(jnp.where(first, entry, earlier))
    own = jnp.where(first, earlier, entry)
    return jnp.concatenate([jnp.where(first, own, got), jnp.where(first, got, own)], 0)


def gather_tokens(x):
    parts = [x]
    for dx, dz in ((0, 1), (1, 0), (3, 0), (1, 1), (3, 1), (2, 0), (2, 1)):
        pairs = [
            (a * 2 + b, ((a + dx) % 4) * 2 + (b + dz) % 2) for a in range(4) for b in range(2)
        ]
        parts.append(lax.ppermute(x, DP, pairs))
    return jnp.concatenate(parts, 0)


def shards(c_guess, adj_guess, norm_gain, w_up, w_down, coarse_rate):
    position = lax.axis_index(LAYER)
    leading = position == 0
    trailing = position == lax.axis_size(LAYER) - 1
    part = lax.axis_index(DP)
    start = c_guess[0]
    guess = adj_guess[0]
    decay = coarse_rate[0]
    gains, ups, downs = norm_gain, w_up, w_down

    end = layer_forward(start, gains[0], ups[0], downs[0])
    end = layer_forward(end, gains[1], ups[1], downs[1])
    shift = jnp.where(leading, end, end - decay * start)
    carried, rates = forward_sweep(decay, shift)
    point = jnp.where(leading, start, carried)

    all_points = gather_tokens(point.astype(bf16))

    (unit0, inv0, _, _, slope0), (unit1, inv1, _, _, slope1) = forward_states(
        point, gains, ups, downs
    )
    out_grad = (step_length * guess).astype(bf16)
    pre_grad = (dot_t(out_grad, downs[1]) * slope1).astype(bf16)
    cot = input_cotangent(guess, dot_t(pre_grad, ups[1]), unit1, inv1, gains[1])
    out_grad = (step_length * cot).astype(bf16)
    pre_grad = (dot_t(out_grad, downs[0]) * slope0).astype(bf16)
    begin = input_cotangent(cot, dot_t(pre_grad, ups[0]), unit0, inv0, gains[0])
    shift = jnp.where(trailing, begin, begin - decay * guess)
    carried = backward_sweep(rates, shift)
    adjoint = jnp.where(trailing, guess, carried)

    all_adj = gather_tokens(adjoint.astype(bf16)).astype(f32)

    (_, _, normed0, hidden0, slope0), (unit1, inv1, normed1, hidden1, slope1) = forward_states(
        all_points.astype(f32), gains, ups, downs
    )
    width_part = normed0.shape[1] // 8
    ff_part = hidden0.shape[1] // 8
    normed0 = lax.dynamic_slice_in_dim(normed0, part * width_part, width_part, 1)
    normed1 = lax.dynamic_slice_in_dim(normed1, part * width_part, width_part, 1)
    hidden0 = lax.dynamic_slice_in_dim(hidden0, part * ff_part, ff_part, 1)
    hidden1 = lax.dynamic_slice_in_dim(hidden1, part * ff_part, ff_part, 1)
    slope0, slope1 = slope0.astype(bf16), slope1.astype(bf16)

    out_grad1 = (step_length * all_adj).astype(bf16)
    pre_grad1 = (dot_t(out_grad1, downs[1]) * slope1).astype(bf16)
    cot = input_cotangent(all_adj, dot_t(pre_grad1, ups[1]), unit1, inv1, gains[1])
    out_grad0 = (step_length * cot).astype(bf16)
    pre_grad0 = (dot_t(out_grad0, downs[0]) * slope0).astype(bf16)
    up_grad = jnp.stack([dot_tokens(normed0, pre_grad0), dot_tokens(normed1, pre_grad1)])
    down_grad = jnp.stack([dot_tokens(hidden0, out_grad0), dot_tokens(hidden1, out_grad1)])
    return (point[None], adjoint[None], up_grad, down_grad)


def solution(mesh):
    finer = Mesh(mesh.devices.reshape(4, 4, 2, 4, 2), LAYER + DP)
    placed = (
        P(LAYER, DP, None),
        P(LAYER, DP, None),
        P(LAYER, None),
        P(LAYER, None, None),
        P(LAYER, None, None),
        P(LAYER, None),
    )
    outs = (P(LAYER, DP, None),) * 4
    return jax.shard_map(shards, mesh=finer, in_specs=placed, out_specs=outs, check_vma=False)
```

```python
import jax
import jax.numpy as jnp
from jax import lax
from jax.experimental import pallas as pl
from jax.experimental.pallas import tpu as pltpu
from jax.sharding import Mesh
from jax.sharding import PartitionSpec as P

LAYER = ("y", "zh", "c")
DP = ("x", "zl")

eps = 1e-06
step_length = 0.5
f32 = jnp.float32
bf16 = jnp.bfloat16
CHUNK = 512
BLOCK = 256
VMEM = pl.BlockSpec(memory_space=pltpu.VMEM)
HBM = pl.BlockSpec(memory_space=pltpu.HBM)
SMEM = pl.BlockSpec(memory_space=pltpu.SMEM)


def dot(a, b):
    return jnp.dot(a, b, preferred_element_type=f32)


def dot_t(a, b):
    return lax.dot_general(a, b, (((1,), (1,)), ((), ())), preferred_element_type=f32)


def dot_tokens(a, b):
    return lax.dot_general(a, b, (((0,), (0,)), ((), ())), preferred_element_type=f32)


def normalize(state):
    inverse_rms = lax.rsqrt(jnp.mean(state * state, axis=-1, keepdims=True) + eps)
    return state * inverse_rms, inverse_rms


def silu_parts(preact):
    s = 0.5 + 0.5 * jnp.tanh(0.5 * preact)
    hidden = preact * s
    return hidden, s + (hidden - hidden * s)


def input_cotangent(cotangent, normed_grad, unit, inverse_rms, gain):
    unit_grad = normed_grad * gain
    inner = jnp.mean(unit_grad * unit, axis=-1, keepdims=True)
    return cotangent + inverse_rms * (unit_grad - unit * inner)


def weight_copies(up_hbm, down_hbm, up, down, sems, wanted):
    copies = {}
    for n, (kind, layer) in enumerate(wanted):
        src, dst = (up_hbm, up) if kind == "up" else (down_hbm, down)
        copies[kind, layer] = pltpu.make_async_copy(src.at[layer], dst.at[layer], sems.at[n])
    return copies


def chunks(width):
    return [slice(n, n + CHUNK) for n in range(0, width, CHUNK)]


def relax_forward(start, gain, rate, up_hbm, down_hbm, shift, up, down, hidden, sems):
    wanted = [("up", 0), ("down", 0), ("up", 1), ("down", 1)]
    copies = weight_copies(up_hbm, down_hbm, up, down, sems, wanted)
    for copy in copies.values():
        copy.start()
    state = start[...]
    for layer in (0, 1):
        unit, _ = normalize(state)
        normed = (unit * gain[layer : layer + 1]).astype(bf16)
        copies["up", layer].wait()
        for cols in chunks(hidden.shape[1]):
            h, _ = silu_parts(dot(normed, up[layer, :, cols]))
            hidden[:, cols] = h.astype(bf16)
        copies["down", layer].wait()
        state = state + step_length * dot(hidden[...], down[layer])
    shift[...] = state - rate[...] * start[...]


def relax_adjoint(
    point, guess, gain, rate, up_hbm, down_hbm, shift, up, down, hidden, slope, pre_grad, sems
):
    wanted = [("up", 0), ("down", 0), ("up", 1), ("down", 1)]
    copies = weight_copies(up_hbm, down_hbm, up, down, sems, wanted)
    for copy in copies.values():
        copy.start()
    ff = chunks(hidden.shape[1])
    g0, g1 = gain[0:1], gain[1:2]
    unit0, inv0 = normalize(point[...])
    normed = (unit0 * g0).astype(bf16)
    copies["up", 0].wait()
    for cols in ff:
        h, sl = silu_parts(dot(normed, up[0, :, cols]))
        hidden[:, cols] = h.astype(bf16)
        slope[:, cols] = sl
    copies["down", 0].wait()
    state = point[...] + step_length * dot(hidden[...], down[0])
    unit1, inv1 = normalize(state)
    normed = (unit1 * g1).astype(bf16)
    out_grad = (step_length * guess[...]).astype(bf16)
    copies["up", 1].wait()
    copies["down", 1].wait()
    for cols in ff:
        _, sl = silu_parts(dot(normed, up[1, :, cols]))
        pre_grad[:, cols] = (dot_t(out_grad, down[1, cols, :]) * sl).astype(bf16)
    cot = input_cotangent(guess[...], dot_t(pre_grad[...], up[1]), unit1, inv1, g1)
    out_grad = (step_length * cot).astype(bf16)
    for cols in ff:
        pre_grad[:, cols] = (dot_t(out_grad, down[0, cols, :]) * slope[:, cols]).astype(bf16)
    begin = input_cotangent(cot, dot_t(pre_grad[...], up[0]), unit0, inv0, g0)
    shift[...] = begin - rate[...] * guess[...]


def forward_parts(
    part, points, gain, up_hbm, down_hbm,
    slope0, slope1, state1, normed0, normed1, hidden0, hidden1,
    up, down, hidden, sems,
):
    first = pl.program_id(0) == 0
    wanted = [("up", 0), ("down", 0), ("up", 1)]
    copies = weight_copies(up_hbm, down_hbm, up, down, sems, wanted)

    @pl.when(first)
    def _():
        for copy in copies.values():
            copy.start()

    def ready(key):
        @pl.when(first)
        def _():
            copies[key].wait()

    me = part[0]
    ff = chunks(hidden.shape[1])
    width = gain.shape[1]
    ff_own = pl.ds(pl.multiple_of(me * 256, 256), 256)
    rows = lax.broadcasted_iota(jnp.int32, (normed0.shape[0], width), 0)
    cols_of = lax.broadcasted_iota(jnp.int32, (normed0.shape[0], width), 1)
    pick = jnp.where(cols_of == rows + me * normed0.shape[0], 1.0, 0.0).astype(bf16)
    point = points[...].astype(f32)
    unit, _ = normalize(point)
    normed = (unit * gain[0:1]).astype(bf16)
    normed0[...] = dot_t(pick, normed).astype(bf16)
    ready(("up", 0))
    for cols in ff:
        h, sl = silu_parts(dot(normed, up[0, :, cols]))
        hidden[:, cols] = h.astype(bf16)
        slope0[:, cols] = sl.astype(bf16)
    hidden0[...] = hidden[:, ff_own]
    ready(("down", 0))
    state = point + step_length * dot(hidden[...], down[0])
    state1[...] = state.astype(bf16)
    unit, _ = normalize(state)
    normed = (unit * gain[1:2]).astype(bf16)
    normed1[...] = dot_t(pick, normed).astype(bf16)
    ready(("up", 1))
    for cols in ff:
        h, sl = silu_parts(dot(normed, up[1, :, cols]))
        hidden[:, cols] = h.astype(bf16)
        slope1[:, cols] = sl.astype(bf16)
    hidden1[...] = hidden[:, ff_own]


def backward_parts(
    adj, gain, slope0, slope1, state1, normed0, normed1, hidden0, hidden1,
    up_hbm, down_hbm, up_old, down_old,
    up_grad, down_grad, up, down, pre_grad, sems,
):
    first = pl.program_id(0) == 0
    wanted = [("down", 1), ("up", 1), ("down", 0)]
    copies = weight_copies(up_hbm, down_hbm, up, down, sems, wanted)

    @pl.when(first)
    def _():
        for copy in copies.values():
            copy.start()
        if up_old is None:
            up_grad[...] = jnp.zeros_like(up_grad)
            down_grad[...] = jnp.zeros_like(down_grad)
        else:
            up_grad[...] = up_old[...]
            down_grad[...] = down_old[...]

    def ready(key):
        @pl.when(first)
        def _():
            copies[key].wait()

    ff = chunks(pre_grad.shape[1])
    cot = adj[...].astype(f32)
    out_grad = (step_length * cot).astype(bf16)
    ready(("down", 1))
    for cols in ff:
        pg = (dot_t(out_grad, down[1, cols, :]) * slope1[:, cols].astype(f32)).astype(bf16)
        pre_grad[:, cols] = pg
        up_grad[1, :, cols] += dot(normed1[...], pg)
    down_grad[1] += dot_tokens(hidden1[...], out_grad)
    unit, inv = normalize(state1[...].astype(f32))
    ready(("up", 1))
    cot = input_cotangent(cot, dot_t(pre_grad[...], up[1]), unit, inv, gain[1:2])
    out_grad = (step_length * cot).astype(bf16)
    ready(("down", 0))
    for cols in ff:
        pg = (dot_t(out_grad, down[0, cols, :]) * slope0[:, cols].astype(f32)).astype(bf16)
        up_grad[0, :, cols] += dot(normed0[...], pg)
    down_grad[0] += dot_tokens(hidden0[...], out_grad)


def backward_parts_first(adj, gain, s0, s1, st, n0, n1, h0, h1, uh, dh, *rest):
    backward_parts(adj, gain, s0, s1, st, n0, n1, h0, h1, uh, dh, None, None, *rest)


def shape(dims, dtype):
    return jax.ShapeDtypeStruct(dims, dtype)


def cost(tokens, matmuls):
    flops = int(2 * tokens * 512 * 2048 * matmuls)
    return pl.CostEstimate(flops=flops, bytes_accessed=8 << 20, transcendentals=0)


def weight_scratch(up, down, n):
    return [pltpu.VMEM(up.shape, bf16), pltpu.VMEM(down.shape, bf16)], [pltpu.SemaphoreType.DMA((n,))]


def call_relax_forward(start, gain, rate, up, down):
    tokens, width = start.shape
    ff = up.shape[2]
    weights, sems = weight_scratch(up, down, 4)
    return pl.pallas_call(
        relax_forward,
        out_shape=shape((tokens, width), f32),
        in_specs=[VMEM, VMEM, VMEM, HBM, HBM],
        out_specs=VMEM,
        scratch_shapes=[*weights, pltpu.VMEM((tokens, ff), bf16), *sems],
        compiler_params=pltpu.CompilerParams(vmem_limit_bytes=60 << 20),
        cost_estimate=cost(tokens, 4),
        name="relax_forward",
    )(start, gain, rate, up, down)


def call_relax_adjoint(point, guess, gain, rate, up, down):
    tokens, width = point.shape
    ff = up.shape[2]
    weights, sems = weight_scratch(up, down, 4)
    return pl.pallas_call(
        relax_adjoint,
        out_shape=shape((tokens, width), f32),
        in_specs=[VMEM, VMEM, VMEM, VMEM, HBM, HBM],
        out_specs=VMEM,
        scratch_shapes=[
            *weights,
            pltpu.VMEM((tokens, ff), bf16),
            pltpu.VMEM((tokens, ff), f32),
            pltpu.VMEM((tokens, ff), bf16),
            *sems,
        ],
        compiler_params=pltpu.CompilerParams(vmem_limit_bytes=60 << 20),
        cost_estimate=cost(tokens, 7),
        name="relax_adjoint",
    )(point, guess, gain, rate, up, down)


def by_rows(width):
    return pl.BlockSpec((BLOCK, width), lambda i: (i, 0))


def by_cols(rows):
    return pl.BlockSpec((rows, BLOCK), lambda i: (0, i))


def whole(dims):
    return pl.BlockSpec(dims, lambda i: (0,) * len(dims))


def call_forward_parts(part, points, gain, up, down):
    tokens, width = points.shape
    ff = up.shape[2]
    weights, sems = weight_scratch(up, down, 3)
    own = ff // 8
    return pl.pallas_call(
        forward_parts,
        grid=(tokens // BLOCK,),
        out_shape=(
            shape((tokens, ff), bf16), shape((tokens, ff), bf16), shape((tokens, width), bf16),
            shape((width // 8, tokens), bf16), shape((width // 8, tokens), bf16),
            shape((tokens, own), bf16), shape((tokens, own), bf16),
        ),
        in_specs=[SMEM, by_rows(width), whole(gain.shape), HBM, HBM],
        out_specs=(
            by_rows(ff), by_rows(ff), by_rows(width), by_cols(width // 8), by_cols(width // 8),
            by_rows(own), by_rows(own),
        ),
        scratch_shapes=[*weights, pltpu.VMEM((BLOCK, ff), bf16), *sems],
        compiler_params=pltpu.CompilerParams(
            vmem_limit_bytes=60 << 20, dimension_semantics=("arbitrary",)
        ),
        cost_estimate=cost(tokens, 3),
        name="forward_parts",
    )(part, points, gain, up, down)


def call_backward_parts(adj, gain, parts, up, down, old=None):
    tokens, width = adj.shape
    ff = up.shape[2]
    weights, sems = weight_scratch(up, down, 3)
    own = ff // 8
    up_dims, down_dims = (2, width // 8, ff), (2, own, width)
    more = [] if old is None else [whole(up_dims), whole(down_dims)]
    return pl.pallas_call(
        backward_parts_first if old is None else backward_parts,
        grid=(tokens // BLOCK,),
        out_shape=(shape(up_dims, f32), shape(down_dims, f32)),
        in_specs=[
            by_rows(width), whole(gain.shape), by_rows(ff), by_rows(ff), by_rows(width),
            by_cols(width // 8), by_cols(width // 8), by_rows(own), by_rows(own), HBM, HBM, *more,
        ],
        out_specs=(whole(up_dims), whole(down_dims)),
        scratch_shapes=[*weights, pltpu.VMEM((BLOCK, ff), bf16), *sems],
        compiler_params=pltpu.CompilerParams(
            vmem_limit_bytes=60 << 20, dimension_semantics=("arbitrary",)
        ),
        cost_estimate=cost(tokens, 3.5),
        name="backward_parts",
    )(adj, gain, *parts, up, down, *(old or ()))


def shift_pairs(size, k):
    return [(i, (i + k) % size) for i in range(size)]


def split_rows(a):
    hi = a.astype(bf16)
    lo = (a - hi.astype(f32)).astype(bf16)
    return hi, lo


def exchange_cores(x):
    return lax.ppermute(x, "c", [(0, 1), (1, 0)])


def line_exchange(payload, axis):
    return [lax.ppermute(payload, axis, shift_pairs(4, k)) for k in (1, 2, 3)]


def pack(rate, shift):
    hi, lo = split_rows(rate)
    pad = jnp.zeros((14, rate.shape[-1]), bf16)
    return jnp.concatenate([shift.astype(bf16), hi, lo, pad], 0)


def unpack(payload, rows):
    shift = payload[:rows].astype(f32)
    rate = payload[rows : rows + 1].astype(f32) + payload[rows + 1 : rows + 2].astype(f32)
    return rate, shift


def fold(pieces, carry, rate, mask, order):
    for k in order:
        a, b = pieces[k - 1]
        keep = mask(k)
        carry = jnp.where(keep, a * carry + b, carry)
        rate = jnp.where(keep, a * rate, rate)
    return rate, carry


def forward_sweep(decay, shift):
    c = lax.axis_index("c")
    zh = lax.axis_index("zh")
    y = lax.axis_index("y")
    half = shift.shape[0] // 2
    first = c == 0
    width = shift.shape[1]
    low, high = shift[:half], shift[half:]
    mine = jnp.where(first, low, high)
    give = jnp.concatenate(
        [jnp.where(first, high, low), jnp.broadcast_to(decay[None], (8, width))], 0
    )
    got = exchange_cores(give)
    other, other_rate = got[:half], got[half : half + 1]
    rate0 = jnp.where(first, decay[None], other_rate)
    rate1 = jnp.where(first, other_rate, decay[None])
    b0 = jnp.where(first, mine, other)
    b1 = jnp.where(first, other, mine)
    pair = (rate0 * rate1, rate1 * b0 + b1)
    pieces_z = [unpack(p, half) for p in line_exchange(pack(*pair), "zh")]
    one = jnp.ones_like(rate0)
    zero = jnp.zeros_like(b0)
    before_rate, before = fold(pieces_z, zero, one, lambda k: zh >= k, (3, 2, 1))
    row = (pair[0] * before_rate, pair[0] * before + pair[1])
    row = fold(pieces_z, row[1], row[0], lambda k: zh < k, (3, 2, 1))
    pieces_y = [unpack(p, half) for p in line_exchange(pack(*row), "y")]
    _, rows_before = fold(pieces_y, zero, one, lambda k: y >= k, (3, 2, 1))
    entry = before_rate * rows_before + before
    later = rate0 * entry + b0
    got = exchange_cores(jnp.where(first, later, entry))
    own = jnp.where(first, entry, later)
    point = jnp.concatenate([jnp.where(first, own, got), jnp.where(first, got, own)], 0)
    rates = (rate0, rate1, [p[0] for p in pieces_z], [p[0] for p in pieces_y])
    return point, rates


def backward_sweep(rates, shift):
    rate0, rate1, rates_z, rates_y = rates
    c = lax.axis_index("c")
    zh = lax.axis_index("zh")
    y = lax.axis_index("y")
    half = shift.shape[0] // 2
    first = c == 0
    low, high = shift[:half], shift[half:]
    mine = jnp.where(first, low, high)
    other = exchange_cores(jnp.where(first, high, low))
    b0 = jnp.where(first, mine, other)
    b1 = jnp.where(first, other, mine)
    pair_rate, pair = rate0 * rate1, rate0 * b1 + b0
    got = line_exchange(pair.astype(bf16), "zh")
    pieces_z = [(a, p.astype(f32)) for a, p in zip(rates_z, got)]
    one = jnp.ones_like(rate0)
    zero = jnp.zeros_like(b0)
    after_rate, after = fold(pieces_z, zero, one, lambda k: zh < k, (1, 2, 3))
    _, row = fold(pieces_z, pair_rate * after + pair, one, lambda k: zh >= k, (1, 2, 3))
    got = line_exchange(row.astype(bf16), "y")
    pieces_y = [(a, p.astype(f32)) for a, p in zip(rates_y, got)]
    _, rows_after = fold(pieces_y, zero, one, lambda k: y < k, (1, 2, 3))
    entry = after_rate * rows_after + after
    earlier = rate1 * entry + b1
    got = exchange_cores(jnp.where(first, entry, earlier))
    own = jnp.where(first, earlier, entry)
    return jnp.concatenate([jnp.where(first, own, got), jnp.where(first, got, own)], 0)


def send(x, axes, dx, dz=None):
    if dz is None:
        return lax.ppermute(x, "x", shift_pairs(4, dx))
    pairs = [(a * 2 + b, (a + dx) % 4 * 2 + (b + dz) % 2) for a in range(4) for b in range(2)]
    return lax.ppermute(x, DP, pairs)


def gather_points(x):
    beside = send(x, DP, 0, 1)
    both = jnp.concatenate([x, beside], 0)
    before, after, across = send(both, "x", 1), send(both, "x", 3), send(both, "x", 2)
    h = x.shape[0] // 2
    far = [across[:h], across[2 * h : 3 * h], across[h : 2 * h], across[3 * h :]]
    return both, jnp.concatenate([before, after], 0), jnp.concatenate(far, 0)


def gather_adjoints(x):
    h = x.shape[0] // 2
    beside = send(x, DP, 0, 1)
    before, after = send(x, "x", 1), send(x, "x", 3)
    before_beside, after_beside = send(x, DP, 1, 1), send(x, DP, 3, 1)
    up = send(jnp.concatenate([before[:h], before_beside[:h]], 0), "x", 1)
    down = send(jnp.concatenate([after[h:], after_beside[h:]], 0), "x", 3)
    near = [x, beside, before, before_beside, after, after_beside]
    return jnp.concatenate(near, 0), jnp.concatenate([up, down], 0)


def shards(c_guess, adj_guess, norm_gain, w_up, w_down, coarse_rate):
    position = lax.axis_index(LAYER)
    leading = position == 0
    trailing = position == lax.axis_size(LAYER) - 1
    part = lax.axis_index(DP).astype(jnp.int32)[None]
    start = c_guess[0]
    guess = adj_guess[0]
    decay = coarse_rate[0]
    rate = decay[None]

    shift = call_relax_forward(start, norm_gain, jnp.where(leading, 0.0, rate), w_up, w_down)
    carried, rates = forward_sweep(decay, shift)
    point = jnp.where(leading, start, carried)
    points_a, points_b, points_c = gather_points(point.astype(bf16))

    shift = call_relax_adjoint(
        point, guess, norm_gain, jnp.where(trailing, 0.0, rate), w_up, w_down
    )
    carried = backward_sweep(rates, shift)
    adjoint = jnp.where(trailing, guess, carried)
    near, far = gather_adjoints(adjoint.astype(bf16))

    parts_near = call_forward_parts(
        part, jnp.concatenate([points_a, points_b], 0), norm_gain, w_up, w_down
    )
    parts_far = call_forward_parts(part, points_c, norm_gain, w_up, w_down)
    sums = call_backward_parts(near, norm_gain, parts_near, w_up, w_down)
    up_grad, down_grad = call_backward_parts(far, norm_gain, parts_far, w_up, w_down, sums)
    return (point[None], adjoint[None], up_grad, down_grad)


def solution(mesh):
    finer = Mesh(mesh.devices.reshape(4, 4, 2, 4, 2), LAYER + DP)
    placed = (
        P(LAYER, DP, None),
        P(LAYER, DP, None),
        P(LAYER, None),
        P(LAYER, None, None),
        P(LAYER, None, None),
        P(LAYER, None),
    )
    outs = (P(LAYER, DP, None),) * 4
    return jax.shard_map(shards, mesh=finer, in_specs=placed, out_specs=outs, check_vma=False)
```

```python
import jax
import jax.numpy as jnp
from jax import lax
from jax.experimental import pallas as pl
from jax.experimental.pallas import tpu as pltpu
from jax.sharding import Mesh
from jax.sharding import PartitionSpec as P

LAYER = ("y", "zh", "c")
DP = ("x", "zl")

eps = 1e-06
step_length = 0.5
f32 = jnp.float32
bf16 = jnp.bfloat16
CHUNK = 512
BLOCK = 256
VMEM = pl.BlockSpec(memory_space=pltpu.VMEM)
ANY = pl.BlockSpec(memory_space=pl.ANY)
SMEM = pl.BlockSpec(memory_space=pltpu.SMEM)


def dot(a, b):
    return jnp.dot(a, b, preferred_element_type=f32)


def dot_t(a, b):
    return lax.dot_general(a, b, (((1,), (1,)), ((), ())), preferred_element_type=f32)


def dot_tokens(a, b):
    return lax.dot_general(a, b, (((0,), (0,)), ((), ())), preferred_element_type=f32)


def normalize(state):
    inverse_rms = lax.rsqrt(jnp.mean(state * state, axis=-1, keepdims=True) + eps)
    return state * inverse_rms, inverse_rms


def silu_parts(preact):
    s = 0.5 + 0.5 * jnp.tanh(0.5 * preact)
    hidden = preact * s
    return hidden, s + (hidden - hidden * s)


def input_cotangent(cotangent, normed_grad, unit, inverse_rms, gain):
    unit_grad = normed_grad * gain
    inner = jnp.mean(unit_grad * unit, axis=-1, keepdims=True)
    return cotangent + inverse_rms * (unit_grad - unit * inner)


def weight_copies(up_hbm, down_hbm, up, down, sems, wanted):
    copies = {}
    for n, (kind, layer) in enumerate(wanted):
        src, dst = (up_hbm, up) if kind == "up" else (down_hbm, down)
        copies[kind, layer] = pltpu.make_async_copy(src.at[layer], dst.at[layer], sems.at[n])
    return copies


def chunks(width):
    return [slice(n, n + CHUNK) for n in range(0, width, CHUNK)]


def relax_forward(start, gain, rate, up_hbm, down_hbm, shift, up, down, hidden, sems):
    wanted = [("up", 0), ("down", 0), ("up", 1), ("down", 1)]
    copies = weight_copies(up_hbm, down_hbm, up, down, sems, wanted)
    for copy in copies.values():
        copy.start()
    state = start[...]
    for layer in (0, 1):
        unit, _ = normalize(state)
        normed = (unit * gain[layer : layer + 1]).astype(bf16)
        copies["up", layer].wait()
        for cols in chunks(hidden.shape[1]):
            h, _ = silu_parts(dot(normed, up[layer, :, cols]))
            hidden[:, cols] = h.astype(bf16)
        copies["down", layer].wait()
        state = state + step_length * dot(hidden[...], down[layer])
    shift[...] = state - rate[...] * start[...]


def relax_adjoint(
    point, guess, gain, rate, up_hbm, down_hbm, shift, up, down, hidden, slope, pre_grad, sems
):
    wanted = [("up", 0), ("down", 0), ("up", 1), ("down", 1)]
    copies = weight_copies(up_hbm, down_hbm, up, down, sems, wanted)
    for copy in copies.values():
        copy.start()
    ff = chunks(hidden.shape[1])
    g0, g1 = gain[0:1], gain[1:2]
    unit0, inv0 = normalize(point[...])
    normed = (unit0 * g0).astype(bf16)
    copies["up", 0].wait()
    for cols in ff:
        h, sl = silu_parts(dot(normed, up[0, :, cols]))
        hidden[:, cols] = h.astype(bf16)
        slope[:, cols] = sl
    copies["down", 0].wait()
    state = point[...] + step_length * dot(hidden[...], down[0])
    unit1, inv1 = normalize(state)
    normed = (unit1 * g1).astype(bf16)
    out_grad = (step_length * guess[...]).astype(bf16)
    copies["up", 1].wait()
    copies["down", 1].wait()
    for cols in ff:
        _, sl = silu_parts(dot(normed, up[1, :, cols]))
        pre_grad[:, cols] = (dot_t(out_grad, down[1, cols, :]) * sl).astype(bf16)
    cot = input_cotangent(guess[...], dot_t(pre_grad[...], up[1]), unit1, inv1, g1)
    out_grad = (step_length * cot).astype(bf16)
    for cols in ff:
        pre_grad[:, cols] = (dot_t(out_grad, down[0, cols, :]) * slope[:, cols]).astype(bf16)
    begin = input_cotangent(cot, dot_t(pre_grad[...], up[0]), unit0, inv0, g0)
    shift[...] = begin - rate[...] * guess[...]


def forward_parts(
    part, points, gain, up_hbm, down_hbm,
    slope0, slope1, state1, normed0, normed1, hidden0, hidden1,
    up, down, hidden, sems,
):
    first = pl.program_id(0) == 0
    wanted = [("up", 0), ("down", 0), ("up", 1)]
    copies = weight_copies(up_hbm, down_hbm, up, down, sems, wanted)

    @pl.when(first)
    def _():
        for copy in copies.values():
            copy.start()

    def ready(key):
        @pl.when(first)
        def _():
            copies[key].wait()

    me = part[0]
    steps = hidden.shape[1] // CHUNK
    width = gain.shape[1]
    ff_own = pl.ds(pl.multiple_of(me * 256, 256), 256)
    rows = lax.broadcasted_iota(jnp.int32, (normed0.shape[0], width), 0)
    cols_of = lax.broadcasted_iota(jnp.int32, (normed0.shape[0], width), 1)
    pick = jnp.where(cols_of == rows + me * normed0.shape[0], 1.0, 0.0).astype(bf16)
    point = points[...].astype(f32)
    unit, _ = normalize(point)
    normed = (unit * gain[0:1]).astype(bf16)
    normed0[...] = dot_t(pick, normed).astype(bf16)
    ready(("up", 0))
    @pl.loop(0, steps)
    def _(n):
        cols = pl.ds(pl.multiple_of(n * CHUNK, CHUNK), CHUNK)
        h, sl = silu_parts(dot(normed, up[0, :, cols]))
        hidden[:, cols] = h.astype(bf16)
        slope0[:, cols] = sl.astype(bf16)

    hidden0[...] = hidden[:, ff_own]
    ready(("down", 0))
    state = point + step_length * dot(hidden[...], down[0])
    state1[...] = state.astype(bf16)
    unit, _ = normalize(state)
    normed = (unit * gain[1:2]).astype(bf16)
    normed1[...] = dot_t(pick, normed).astype(bf16)
    ready(("up", 1))
    @pl.loop(0, steps)
    def _(n):
        cols = pl.ds(pl.multiple_of(n * CHUNK, CHUNK), CHUNK)
        h, sl = silu_parts(dot(normed, up[1, :, cols]))
        hidden[:, cols] = h.astype(bf16)
        slope1[:, cols] = sl.astype(bf16)

    hidden1[...] = hidden[:, ff_own]


def backward_parts(
    adj, gain, slope0, slope1, state1, normed0, normed1, hidden0, hidden1,
    up_hbm, down_hbm, up_old, down_old,
    up_grad, down_grad, up, down, pre_grad, sems,
):
    first = pl.program_id(0) == 0
    wanted = [("down", 1), ("up", 1), ("down", 0)]
    copies = weight_copies(up_hbm, down_hbm, up, down, sems, wanted)

    @pl.when(first)
    def _():
        for copy in copies.values():
            copy.start()
        if up_old is None:
            up_grad[...] = jnp.zeros_like(up_grad)
            down_grad[...] = jnp.zeros_like(down_grad)
        else:
            up_grad[...] = up_old[...]
            down_grad[...] = down_old[...]

    def ready(key):
        @pl.when(first)
        def _():
            copies[key].wait()

    steps = pre_grad.shape[1] // CHUNK
    cot = adj[...].astype(f32)
    out_grad = (step_length * cot).astype(bf16)
    ready(("down", 1))
    @pl.loop(0, steps)
    def _(n):
        cols = pl.ds(pl.multiple_of(n * CHUNK, CHUNK), CHUNK)
        pg = (dot_t(out_grad, down[1, cols, :]) * slope1[:, cols].astype(f32)).astype(bf16)
        pre_grad[:, cols] = pg
        up_grad[1, :, cols] += dot(normed1[...], pg)

    down_grad[1] += dot_tokens(hidden1[...], out_grad)
    unit, inv = normalize(state1[...].astype(f32))
    ready(("up", 1))
    cot = input_cotangent(cot, dot_t(pre_grad[...], up[1]), unit, inv, gain[1:2])
    out_grad = (step_length * cot).astype(bf16)
    ready(("down", 0))
    @pl.loop(0, steps)
    def _(n):
        cols = pl.ds(pl.multiple_of(n * CHUNK, CHUNK), CHUNK)
        pg = (dot_t(out_grad, down[0, cols, :]) * slope0[:, cols].astype(f32)).astype(bf16)
        up_grad[0, :, cols] += dot(normed0[...], pg)

    down_grad[0] += dot_tokens(hidden0[...], out_grad)


def backward_parts_first(adj, gain, s0, s1, st, n0, n1, h0, h1, uh, dh, *rest):
    backward_parts(adj, gain, s0, s1, st, n0, n1, h0, h1, uh, dh, None, None, *rest)


def shape(dims, dtype):
    return jax.ShapeDtypeStruct(dims, dtype)


def cost(tokens, matmuls):
    flops = int(2 * tokens * 512 * 2048 * matmuls)
    return pl.CostEstimate(flops=flops, bytes_accessed=8 << 20, transcendentals=0)


def weight_scratch(up, down, n):
    return [pltpu.VMEM(up.shape, bf16), pltpu.VMEM(down.shape, bf16)], [pltpu.SemaphoreType.DMA((n,))]


def call_relax_forward(start, gain, rate, up, down):
    tokens, width = start.shape
    ff = up.shape[2]
    weights, sems = weight_scratch(up, down, 4)
    return pl.pallas_call(
        relax_forward,
        out_shape=shape((tokens, width), f32),
        in_specs=[VMEM, VMEM, VMEM, ANY, ANY],
        out_specs=VMEM,
        scratch_shapes=[*weights, pltpu.VMEM((tokens, ff), bf16), *sems],
        compiler_params=pltpu.CompilerParams(vmem_limit_bytes=24 << 20),
        cost_estimate=cost(tokens, 4),
        name="relax_forward",
    )(start, gain, rate, up, down)


def call_relax_adjoint(point, guess, gain, rate, up, down):
    tokens, width = point.shape
    ff = up.shape[2]
    weights, sems = weight_scratch(up, down, 4)
    return pl.pallas_call(
        relax_adjoint,
        out_shape=shape((tokens, width), f32),
        in_specs=[VMEM, VMEM, VMEM, VMEM, ANY, ANY],
        out_specs=VMEM,
        scratch_shapes=[
            *weights,
            pltpu.VMEM((tokens, ff), bf16),
            pltpu.VMEM((tokens, ff), f32),
            pltpu.VMEM((tokens, ff), bf16),
            *sems,
        ],
        compiler_params=pltpu.CompilerParams(vmem_limit_bytes=24 << 20),
        cost_estimate=cost(tokens, 7),
        name="relax_adjoint",
    )(point, guess, gain, rate, up, down)


def by_rows(width):
    return pl.BlockSpec((BLOCK, width), lambda i: (i, 0))


def by_cols(rows):
    return pl.BlockSpec((rows, BLOCK), lambda i: (0, i))


def whole(dims):
    return pl.BlockSpec(dims, lambda i: (0,) * len(dims))


def call_forward_parts(part, points, gain, up, down):
    tokens, width = points.shape
    ff = up.shape[2]
    weights, sems = weight_scratch(up, down, 3)
    own = ff // 8
    return pl.pallas_call(
        forward_parts,
        grid=(tokens // BLOCK,),
        out_shape=(
            shape((tokens, ff), bf16), shape((tokens, ff), bf16), shape((tokens, width), bf16),
            shape((width // 8, tokens), bf16), shape((width // 8, tokens), bf16),
            shape((tokens, own), bf16), shape((tokens, own), bf16),
        ),
        in_specs=[SMEM, by_rows(width), whole(gain.shape), ANY, ANY],
        out_specs=(
            by_rows(ff), by_rows(ff), by_rows(width), by_cols(width // 8), by_cols(width // 8),
            by_rows(own), by_rows(own),
        ),
        scratch_shapes=[*weights, pltpu.VMEM((BLOCK, ff), bf16), *sems],
        compiler_params=pltpu.CompilerParams(
            vmem_limit_bytes=40 << 20, dimension_semantics=("arbitrary",)
        ),
        cost_estimate=cost(tokens, 3),
        name="forward_parts",
    )(part, points, gain, up, down)


def call_backward_parts(adj, gain, parts, up, down, old=None):
    tokens, width = adj.shape
    ff = up.shape[2]
    weights, sems = weight_scratch(up, down, 3)
    own = ff // 8
    up_dims, down_dims = (2, width // 8, ff), (2, own, width)
    more = [] if old is None else [whole(up_dims), whole(down_dims)]
    return pl.pallas_call(
        backward_parts_first if old is None else backward_parts,
        grid=(tokens // BLOCK,),
        out_shape=(shape(up_dims, f32), shape(down_dims, f32)),
        in_specs=[
            by_rows(width), whole(gain.shape), by_rows(ff), by_rows(ff), by_rows(width),
            by_cols(width // 8), by_cols(width // 8), by_rows(own), by_rows(own), ANY, ANY, *more,
        ],
        out_specs=(whole(up_dims), whole(down_dims)),
        scratch_shapes=[*weights, pltpu.VMEM((BLOCK, ff), bf16), *sems],
        compiler_params=pltpu.CompilerParams(
            vmem_limit_bytes=40 << 20, dimension_semantics=("arbitrary",)
        ),
        cost_estimate=cost(tokens, 3.5),
        name="backward_parts",
    )(adj, gain, *parts, up, down, *(old or ()))


def shift_pairs(size, k):
    return [(i, (i + k) % size) for i in range(size)]


def split_rows(a):
    hi = a.astype(bf16)
    lo = (a - hi.astype(f32)).astype(bf16)
    return hi, lo


def exchange_cores(x):
    return lax.ppermute(x, "c", [(0, 1), (1, 0)])


def line_exchange(payload, axis):
    return [lax.ppermute(payload, axis, shift_pairs(4, k)) for k in (1, 2, 3)]


def pack(rate, shift):
    hi, lo = split_rows(rate)
    pad = jnp.zeros((14, rate.shape[-1]), bf16)
    return jnp.concatenate([shift.astype(bf16), hi, lo, pad], 0)


def unpack(payload, rows):
    shift = payload[:rows].astype(f32)
    rate = payload[rows : rows + 1].astype(f32) + payload[rows + 1 : rows + 2].astype(f32)
    return rate, shift


def fold(pieces, carry, rate, mask, order):
    for k in order:
        a, b = pieces[k - 1]
        keep = mask(k)
        carry = jnp.where(keep, a * carry + b, carry)
        rate = jnp.where(keep, a * rate, rate)
    return rate, carry


def forward_sweep(decay, shift):
    c = lax.axis_index("c")
    zh = lax.axis_index("zh")
    y = lax.axis_index("y")
    half = shift.shape[0] // 2
    first = c == 0
    width = shift.shape[1]
    low, high = shift[:half], shift[half:]
    mine = jnp.where(first, low, high)
    give = jnp.concatenate(
        [jnp.where(first, high, low), jnp.broadcast_to(decay[None], (8, width))], 0
    )
    got = exchange_cores(give)
    other, other_rate = got[:half], got[half : half + 1]
    rate0 = jnp.where(first, decay[None], other_rate)
    rate1 = jnp.where(first, other_rate, decay[None])
    b0 = jnp.where(first, mine, other)
    b1 = jnp.where(first, other, mine)
    pair = (rate0 * rate1, rate1 * b0 + b1)
    pieces_z = [unpack(p, half) for p in line_exchange(pack(*pair), "zh")]
    one = jnp.ones_like(rate0)
    zero = jnp.zeros_like(b0)
    before_rate, before = fold(pieces_z, zero, one, lambda k: zh >= k, (3, 2, 1))
    row = (pair[0] * before_rate, pair[0] * before + pair[1])
    row = fold(pieces_z, row[1], row[0], lambda k: zh < k, (3, 2, 1))
    pieces_y = [unpack(p, half) for p in line_exchange(pack(*row), "y")]
    _, rows_before = fold(pieces_y, zero, one, lambda k: y >= k, (3, 2, 1))
    entry = before_rate * rows_before + before
    later = rate0 * entry + b0
    got = exchange_cores(jnp.where(first, later, entry))
    own = jnp.where(first, entry, later)
    point = jnp.concatenate([jnp.where(first, own, got), jnp.where(first, got, own)], 0)
    rates = (rate0, rate1, [p[0] for p in pieces_z], [p[0] for p in pieces_y])
    return point, rates


def backward_sweep(rates, shift, beside_line, beside_rows):
    rate0, rate1, rates_z, rates_y = rates
    c = lax.axis_index("c")
    zh = lax.axis_index("zh")
    y = lax.axis_index("y")
    half = shift.shape[0] // 2
    first = c == 0
    low, high = shift[:half], shift[half:]
    mine = jnp.where(first, low, high)
    other = exchange_cores(jnp.where(first, high, low))
    b0 = jnp.where(first, mine, other)
    b1 = jnp.where(first, other, mine)
    pair_rate, pair = rate0 * rate1, rate0 * b1 + b0
    sent, kept = beside_line(pair.astype(bf16))
    got = line_exchange(sent, "zh")
    pieces_z = [(a, p.astype(f32)) for a, p in zip(rates_z, got)]
    one = jnp.ones_like(rate0)
    zero = jnp.zeros_like(b0)
    after_rate, after = fold(pieces_z, zero, one, lambda k: zh < k, (1, 2, 3))
    _, row = fold(pieces_z, pair_rate * after + pair, one, lambda k: zh >= k, (1, 2, 3))
    sent, kept = beside_rows(row.astype(bf16), kept)
    got, kept = lax.optimization_barrier((line_exchange(sent, "y"), kept))
    pieces_y = [(a, p.astype(f32)) for a, p in zip(rates_y, got)]
    _, rows_after = fold(pieces_y, zero, one, lambda k: y < k, (1, 2, 3))
    entry = after_rate * rows_after + after
    earlier = rate1 * entry + b1
    got = exchange_cores(jnp.where(first, entry, earlier))
    own = jnp.where(first, earlier, entry)
    carried = jnp.concatenate([jnp.where(first, own, got), jnp.where(first, got, own)], 0)
    return carried, kept


def send(x, axes, dx, dz=None):
    if dz is None:
        return lax.ppermute(x, "x", shift_pairs(4, dx))
    pairs = [(a * 2 + b, (a + dx) % 4 * 2 + (b + dz) % 2) for a in range(4) for b in range(2)]
    return lax.ppermute(x, DP, pairs)


def far_order(x):
    h = x.shape[0] // 4
    return jnp.concatenate([x[:h], x[2 * h : 3 * h], x[h : 2 * h], x[3 * h :]], 0)


def gather_adjoints(x):
    h = x.shape[0] // 2
    beside = send(x, DP, 0, 1)
    before, after = send(x, "x", 1), send(x, "x", 3)
    before_beside, after_beside = send(x, DP, 1, 1), send(x, DP, 3, 1)
    up = send(jnp.concatenate([before[:h], before_beside[:h]], 0), "x", 1)
    down = send(jnp.concatenate([after[h:], after_beside[h:]], 0), "x", 3)
    near = jnp.concatenate([before, before_beside, after, after_beside], 0)
    return jnp.concatenate([x, beside], 0), near, jnp.concatenate([up, down], 0)


def shards(c_guess, adj_guess, norm_gain, w_up, w_down, coarse_rate):
    position = lax.axis_index(LAYER)
    leading = position == 0
    trailing = position == lax.axis_size(LAYER) - 1
    part = lax.axis_index(DP).astype(jnp.int32)[None]
    start = c_guess[0]
    guess = adj_guess[0]
    decay = coarse_rate[0]
    rate = decay[None]
    w_up = pltpu.with_memory_space_constraint(w_up, pltpu.HBM)
    w_down = pltpu.with_memory_space_constraint(w_down, pltpu.HBM)

    shift = call_relax_forward(start, norm_gain, jnp.where(leading, 0.0, rate), w_up, w_down)
    carried, rates = forward_sweep(decay, shift)
    point = jnp.where(leading, start, carried)
    rounded = point.astype(bf16)
    beside = send(rounded, DP, 0, 1)
    shift = call_relax_adjoint(
        point, guess, norm_gain, jnp.where(trailing, 0.0, rate), w_up, w_down
    )
    shift, beside = lax.optimization_barrier((shift, beside))
    both = jnp.concatenate([rounded, beside], 0)

    def forward_of(points):
        return call_forward_parts(part, points, norm_gain, w_up, w_down)

    def beside_line(sent):
        sent, mine = lax.optimization_barrier((sent, both))
        others = [send(mine, "x", k) for k in (1, 3, 2)]
        return sent, (forward_of(mine), others)

    def beside_rows(sent, kept):
        sent, (parts, others) = lax.optimization_barrier((sent, kept))
        return sent, (parts, others[:2], forward_of(far_order(others[2])))

    carried, (parts_own, others, parts_far) = backward_sweep(rates, shift, beside_line, beside_rows)
    adjoint = jnp.where(trailing, guess, carried)
    rounded, others = lax.optimization_barrier((adjoint.astype(bf16), others))
    mine, near, far = gather_adjoints(rounded)
    parts_near = forward_of(jnp.concatenate(others, 0))
    sums = call_backward_parts(mine, norm_gain, parts_own, w_up, w_down)
    sums = call_backward_parts(near, norm_gain, parts_near, w_up, w_down, sums)
    up_grad, down_grad = call_backward_parts(far, norm_gain, parts_far, w_up, w_down, sums)
    return (point[None], adjoint[None], up_grad, down_grad)


def solution(mesh):
    finer = Mesh(mesh.devices.reshape(4, 4, 2, 4, 2), LAYER + DP)
    placed = (
        P(LAYER, DP, None),
        P(LAYER, DP, None),
        P(LAYER, None),
        P(LAYER, None, None),
        P(LAYER, None, None),
        P(LAYER, None),
    )
    outs = (P(LAYER, DP, None),) * 4
    return jax.shard_map(shards, mesh=finer, in_specs=placed, out_specs=outs, check_vma=False)
```

```python
import jax
import jax.numpy as jnp
from jax import lax
from jax.experimental import pallas as pl
from jax.experimental.pallas import tpu as pltpu
from jax.sharding import Mesh
from jax.sharding import PartitionSpec as P

LAYER = ("y", "zh", "c")
DP = ("x", "zl")

eps = 1e-06
step_length = 0.5
f32 = jnp.float32
bf16 = jnp.bfloat16
CHUNK = 512
UNROLL = 2
BLOCK = 256
VMEM = pl.BlockSpec(memory_space=pltpu.VMEM)
ANY = pl.BlockSpec(memory_space=pl.ANY)
SMEM = pl.BlockSpec(memory_space=pltpu.SMEM)


def dot(a, b):
    return jnp.dot(a, b, preferred_element_type=f32)


def dot_t(a, b):
    return lax.dot_general(a, b, (((1,), (1,)), ((), ())), preferred_element_type=f32)


def dot_tokens(a, b):
    return lax.dot_general(a, b, (((0,), (0,)), ((), ())), preferred_element_type=f32)


def normalize(state):
    inverse_rms = lax.rsqrt(jnp.mean(state * state, axis=-1, keepdims=True) + eps)
    return state * inverse_rms, inverse_rms


def silu_parts(preact):
    s = 0.5 + 0.5 * jnp.tanh(0.5 * preact)
    hidden = preact * s
    return hidden, s + (hidden - hidden * s)


def input_cotangent(cotangent, normed_grad, unit, inverse_rms, gain):
    unit_grad = normed_grad * gain
    inner = jnp.mean(unit_grad * unit, axis=-1, keepdims=True)
    return cotangent + inverse_rms * (unit_grad - unit * inner)


def weight_copies(up_hbm, down_hbm, up, down, sems, wanted):
    copies = {}
    for n, (kind, layer) in enumerate(wanted):
        src, dst = (up_hbm, up) if kind == "up" else (down_hbm, down)
        copies[kind, layer] = pltpu.make_async_copy(src.at[layer], dst.at[layer], sems.at[n])
    return copies


def chunks(width):
    return [slice(n, n + CHUNK) for n in range(0, width, CHUNK)]


def relax_forward(start, gain, rate, up_hbm, down_hbm, shift, up, down, hidden, sems):
    wanted = [("up", 0), ("down", 0), ("up", 1), ("down", 1)]
    copies = weight_copies(up_hbm, down_hbm, up, down, sems, wanted)
    for copy in copies.values():
        copy.start()
    state = start[...]
    for layer in (0, 1):
        unit, _ = normalize(state)
        normed = (unit * gain[layer : layer + 1]).astype(bf16)
        copies["up", layer].wait()
        for cols in chunks(hidden.shape[1]):
            h, _ = silu_parts(dot(normed, up[layer, :, cols]))
            hidden[:, cols] = h.astype(bf16)
        copies["down", layer].wait()
        state = state + step_length * dot(hidden[...], down[layer])
    shift[...] = state - rate[...] * start[...]


def relax_adjoint(
    point, guess, gain, rate, up_hbm, down_hbm, shift, up, down, hidden, slope, pre_grad, sems
):
    wanted = [("up", 0), ("down", 0), ("up", 1), ("down", 1)]
    copies = weight_copies(up_hbm, down_hbm, up, down, sems, wanted)
    for copy in copies.values():
        copy.start()
    ff = chunks(hidden.shape[1])
    g0, g1 = gain[0:1], gain[1:2]
    unit0, inv0 = normalize(point[...])
    normed = (unit0 * g0).astype(bf16)
    copies["up", 0].wait()
    for cols in ff:
        h, sl = silu_parts(dot(normed, up[0, :, cols]))
        hidden[:, cols] = h.astype(bf16)
        slope[:, cols] = sl
    copies["down", 0].wait()
    state = point[...] + step_length * dot(hidden[...], down[0])
    unit1, inv1 = normalize(state)
    normed = (unit1 * g1).astype(bf16)
    out_grad = (step_length * guess[...]).astype(bf16)
    copies["up", 1].wait()
    copies["down", 1].wait()
    for cols in ff:
        _, sl = silu_parts(dot(normed, up[1, :, cols]))
        pre_grad[:, cols] = (dot_t(out_grad, down[1, cols, :]) * sl).astype(bf16)
    cot = input_cotangent(guess[...], dot_t(pre_grad[...], up[1]), unit1, inv1, g1)
    out_grad = (step_length * cot).astype(bf16)
    for cols in ff:
        pre_grad[:, cols] = (dot_t(out_grad, down[0, cols, :]) * slope[:, cols]).astype(bf16)
    begin = input_cotangent(cot, dot_t(pre_grad[...], up[0]), unit0, inv0, g0)
    shift[...] = begin - rate[...] * guess[...]


def forward_parts(
    part, points, gain, up, down,
    slope0, slope1, state1, normed0, normed1, hidden0, hidden1,
    hidden,
):
    me = part[0]
    steps = hidden.shape[1] // CHUNK
    width = gain.shape[1]
    ff_own = pl.ds(pl.multiple_of(me * 256, 256), 256)
    rows = lax.broadcasted_iota(jnp.int32, (normed0.shape[0], width), 0)
    cols_of = lax.broadcasted_iota(jnp.int32, (normed0.shape[0], width), 1)
    pick = jnp.where(cols_of == rows + me * normed0.shape[0], 1.0, 0.0).astype(bf16)
    point = points[...].astype(f32)
    unit, _ = normalize(point)
    normed = (unit * gain[0:1]).astype(bf16)
    normed0[...] = dot_t(pick, normed).astype(bf16)
    @pl.loop(0, steps // UNROLL)
    def _(n):
        for k in range(UNROLL):
            cols = pl.ds(pl.multiple_of((n * UNROLL + k) * CHUNK, CHUNK), CHUNK)
            h, sl = silu_parts(dot(normed, up[0, :, cols]))
            hidden[:, cols] = h.astype(bf16)
            slope0[:, cols] = sl.astype(bf16)

    hidden0[...] = hidden[:, ff_own]
    state = point + step_length * dot(hidden[...], down[0])
    state1[...] = state.astype(bf16)
    unit, _ = normalize(state)
    normed = (unit * gain[1:2]).astype(bf16)
    normed1[...] = dot_t(pick, normed).astype(bf16)
    @pl.loop(0, steps // UNROLL)
    def _(n):
        for k in range(UNROLL):
            cols = pl.ds(pl.multiple_of((n * UNROLL + k) * CHUNK, CHUNK), CHUNK)
            h, sl = silu_parts(dot(normed, up[1, :, cols]))
            hidden[:, cols] = h.astype(bf16)
            slope1[:, cols] = sl.astype(bf16)

    hidden1[...] = hidden[:, ff_own]


def backward_parts(
    adj, gain, slope0, slope1, state1, normed0, normed1, hidden0, hidden1,
    up, down, up_old, down_old,
    up_grad, down_grad, pre_grad,
):
    first = pl.program_id(0) == 0

    @pl.when(first)
    def _():
        if up_old is None:
            up_grad[...] = jnp.zeros_like(up_grad)
            down_grad[...] = jnp.zeros_like(down_grad)
        else:
            up_grad[...] = up_old[...]
            down_grad[...] = down_old[...]

    steps = pre_grad.shape[1] // CHUNK
    cot = adj[...].astype(f32)
    out_grad = (step_length * cot).astype(bf16)
    @pl.loop(0, steps // UNROLL)
    def _(n):
        for k in range(UNROLL):
            cols = pl.ds(pl.multiple_of((n * UNROLL + k) * CHUNK, CHUNK), CHUNK)
            pg = (dot_t(out_grad, down[1, cols, :]) * slope1[:, cols].astype(f32)).astype(bf16)
            pre_grad[:, cols] = pg
            up_grad[1, :, cols] += dot(normed1[...], pg)

    down_grad[1] += dot_tokens(hidden1[...], out_grad)
    unit, inv = normalize(state1[...].astype(f32))
    cot = input_cotangent(cot, dot_t(pre_grad[...], up[1]), unit, inv, gain[1:2])
    out_grad = (step_length * cot).astype(bf16)
    @pl.loop(0, steps // UNROLL)
    def _(n):
        for k in range(UNROLL):
            cols = pl.ds(pl.multiple_of((n * UNROLL + k) * CHUNK, CHUNK), CHUNK)
            pg = (dot_t(out_grad, down[0, cols, :]) * slope0[:, cols].astype(f32)).astype(bf16)
            up_grad[0, :, cols] += dot(normed0[...], pg)

    down_grad[0] += dot_tokens(hidden0[...], out_grad)


def backward_parts_first(adj, gain, s0, s1, st, n0, n1, h0, h1, uh, dh, *rest):
    backward_parts(adj, gain, s0, s1, st, n0, n1, h0, h1, uh, dh, None, None, *rest)


def shape(dims, dtype):
    return jax.ShapeDtypeStruct(dims, dtype)


def cost(tokens, matmuls):
    flops = int(2 * tokens * 512 * 2048 * matmuls)
    return pl.CostEstimate(flops=flops, bytes_accessed=8 << 20, transcendentals=0)


def weight_scratch(up, down, n):
    return [pltpu.VMEM(up.shape, bf16), pltpu.VMEM(down.shape, bf16)], [pltpu.SemaphoreType.DMA((n,))]


def call_relax_forward(start, gain, rate, up, down):
    tokens, width = start.shape
    ff = up.shape[2]
    weights, sems = weight_scratch(up, down, 4)
    return pl.pallas_call(
        relax_forward,
        out_shape=shape((tokens, width), f32),
        in_specs=[VMEM, VMEM, VMEM, ANY, ANY],
        out_specs=VMEM,
        scratch_shapes=[*weights, pltpu.VMEM((tokens, ff), bf16), *sems],
        compiler_params=pltpu.CompilerParams(vmem_limit_bytes=24 << 20),
        cost_estimate=cost(tokens, 4),
        name="relax_forward",
    )(start, gain, rate, up, down)


def call_relax_adjoint(point, guess, gain, rate, up, down):
    tokens, width = point.shape
    ff = up.shape[2]
    return pl.pallas_call(
        relax_adjoint,
        out_shape=(
            shape((tokens, width), f32), pltpu.VMEM(up.shape, bf16), pltpu.VMEM(down.shape, bf16),
        ),
        in_specs=[VMEM, VMEM, VMEM, VMEM, ANY, ANY],
        out_specs=(VMEM, VMEM, VMEM),
        scratch_shapes=[
            pltpu.VMEM((tokens, ff), bf16),
            pltpu.VMEM((tokens, ff), f32),
            pltpu.VMEM((tokens, ff), bf16),
            pltpu.SemaphoreType.DMA((4,)),
        ],
        compiler_params=pltpu.CompilerParams(vmem_limit_bytes=16 << 20),
        cost_estimate=cost(tokens, 7),
        name="relax_adjoint",
    )(point, guess, gain, rate, up, down)


def by_rows(width):
    return pl.BlockSpec((BLOCK, width), lambda i: (i, 0))


def by_cols(rows):
    return pl.BlockSpec((rows, BLOCK), lambda i: (0, i))


def whole(dims):
    return pl.BlockSpec(dims, lambda i: (0,) * len(dims))


def call_forward_parts(part, points, gain, up, down):
    tokens, width = points.shape
    ff = up.shape[2]
    own = ff // 8
    return pl.pallas_call(
        forward_parts,
        grid=(tokens // BLOCK,),
        out_shape=(
            shape((tokens, ff), bf16), shape((tokens, ff), bf16), shape((tokens, width), bf16),
            shape((width // 8, tokens), bf16), shape((width // 8, tokens), bf16),
            shape((tokens, own), bf16), shape((tokens, own), bf16),
        ),
        in_specs=[SMEM, by_rows(width), whole(gain.shape), VMEM, VMEM],
        out_specs=(
            by_rows(ff), by_rows(ff), by_rows(width), by_cols(width // 8), by_cols(width // 8),
            by_rows(own), by_rows(own),
        ),
        scratch_shapes=[pltpu.VMEM((BLOCK, ff), bf16)],
        compiler_params=pltpu.CompilerParams(
            vmem_limit_bytes=24 << 20, dimension_semantics=("arbitrary",)
        ),
        cost_estimate=cost(tokens, 3),
        name="forward_parts",
    )(part, points, gain, up, down)


def call_backward_parts(adj, gain, parts, up, down, old=None):
    tokens, width = adj.shape
    ff = up.shape[2]
    own = ff // 8
    up_dims, down_dims = (2, width // 8, ff), (2, own, width)
    more = [] if old is None else [whole(up_dims), whole(down_dims)]
    return pl.pallas_call(
        backward_parts_first if old is None else backward_parts,
        grid=(tokens // BLOCK,),
        out_shape=(shape(up_dims, f32), shape(down_dims, f32)),
        in_specs=[
            by_rows(width), whole(gain.shape), by_rows(ff), by_rows(ff), by_rows(width),
            by_cols(width // 8), by_cols(width // 8), by_rows(own), by_rows(own), VMEM, VMEM, *more,
        ],
        out_specs=(whole(up_dims), whole(down_dims)),
        scratch_shapes=[pltpu.VMEM((BLOCK, ff), bf16)],
        compiler_params=pltpu.CompilerParams(
            vmem_limit_bytes=24 << 20, dimension_semantics=("arbitrary",)
        ),
        cost_estimate=cost(tokens, 3.5),
        name="backward_parts",
    )(adj, gain, *parts, up, down, *(old or ()))


def shift_pairs(size, k):
    return [(i, (i + k) % size) for i in range(size)]


def split_rows(a):
    hi = a.astype(bf16)
    lo = (a - hi.astype(f32)).astype(bf16)
    return hi, lo


def exchange_cores(x):
    return lax.ppermute(x, "c", [(0, 1), (1, 0)])


def line_exchange(payload, axis):
    return [lax.ppermute(payload, axis, shift_pairs(4, k)) for k in (1, 2, 3)]


def pack(rate, shift):
    hi, lo = split_rows(rate)
    pad = jnp.zeros((14, rate.shape[-1]), bf16)
    return jnp.concatenate([shift.astype(bf16), hi, lo, pad], 0)


def unpack(payload, rows):
    shift = payload[:rows].astype(f32)
    rate = payload[rows : rows + 1].astype(f32) + payload[rows + 1 : rows + 2].astype(f32)
    return rate, shift


def fold(pieces, carry, rate, mask, order):
    for k in order:
        a, b = pieces[k - 1]
        keep = mask(k)
        carry = jnp.where(keep, a * carry + b, carry)
        rate = jnp.where(keep, a * rate, rate)
    return rate, carry


def forward_sweep(decay, shift):
    c = lax.axis_index("c")
    zh = lax.axis_index("zh")
    y = lax.axis_index("y")
    half = shift.shape[0] // 2
    first = c == 0
    width = shift.shape[1]
    low, high = shift[:half], shift[half:]
    mine = jnp.where(first, low, high)
    give = jnp.concatenate(
        [jnp.where(first, high, low), jnp.broadcast_to(decay[None], (8, width))], 0
    )
    got = exchange_cores(give)
    other, other_rate = got[:half], got[half : half + 1]
    rate0 = jnp.where(first, decay[None], other_rate)
    rate1 = jnp.where(first, other_rate, decay[None])
    b0 = jnp.where(first, mine, other)
    b1 = jnp.where(first, other, mine)
    pair = (rate0 * rate1, rate1 * b0 + b1)
    pieces_z = [unpack(p, half) for p in line_exchange(pack(*pair), "zh")]
    one = jnp.ones_like(rate0)
    zero = jnp.zeros_like(b0)
    before_rate, before = fold(pieces_z, zero, one, lambda k: zh >= k, (3, 2, 1))
    row = (pair[0] * before_rate, pair[0] * before + pair[1])
    row = fold(pieces_z, row[1], row[0], lambda k: zh < k, (3, 2, 1))
    pieces_y = [unpack(p, half) for p in line_exchange(pack(*row), "y")]
    _, rows_before = fold(pieces_y, zero, one, lambda k: y >= k, (3, 2, 1))
    entry = before_rate * rows_before + before
    later = rate0 * entry + b0
    got = exchange_cores(jnp.where(first, later, entry))
    own = jnp.where(first, entry, later)
    point = jnp.concatenate([jnp.where(first, own, got), jnp.where(first, got, own)], 0)
    rates = (rate0, rate1, [p[0] for p in pieces_z], [p[0] for p in pieces_y])
    return point, rates


def backward_sweep(rates, shift, beside_line, beside_rows):
    rate0, rate1, rates_z, rates_y = rates
    c = lax.axis_index("c")
    zh = lax.axis_index("zh")
    y = lax.axis_index("y")
    half = shift.shape[0] // 2
    first = c == 0
    low, high = shift[:half], shift[half:]
    mine = jnp.where(first, low, high)
    other = exchange_cores(jnp.where(first, high, low))
    b0 = jnp.where(first, mine, other)
    b1 = jnp.where(first, other, mine)
    pair_rate, pair = rate0 * rate1, rate0 * b1 + b0
    sent, kept = beside_line(pair.astype(bf16))
    got = line_exchange(sent, "zh")
    pieces_z = [(a, p.astype(f32)) for a, p in zip(rates_z, got)]
    one = jnp.ones_like(rate0)
    zero = jnp.zeros_like(b0)
    after_rate, after = fold(pieces_z, zero, one, lambda k: zh < k, (1, 2, 3))
    _, row = fold(pieces_z, pair_rate * after + pair, one, lambda k: zh >= k, (1, 2, 3))
    sent, kept = beside_rows(row.astype(bf16), kept)
    got, finished = lax.optimization_barrier((line_exchange(sent, "y"), kept[2]))
    kept = (*kept[:2], finished)
    pieces_y = [(a, p.astype(f32)) for a, p in zip(rates_y, got)]
    _, rows_after = fold(pieces_y, zero, one, lambda k: y < k, (1, 2, 3))
    entry = after_rate * rows_after + after
    earlier = rate1 * entry + b1
    got = exchange_cores(jnp.where(first, entry, earlier))
    own = jnp.where(first, earlier, entry)
    carried = jnp.concatenate([jnp.where(first, own, got), jnp.where(first, got, own)], 0)
    return carried, kept


def send(x, axes, dx, dz=None):
    if dz is None:
        return lax.ppermute(x, "x", shift_pairs(4, dx))
    pairs = [(a * 2 + b, (a + dx) % 4 * 2 + (b + dz) % 2) for a in range(4) for b in range(2)]
    return lax.ppermute(x, DP, pairs)


def far_order(x):
    h = x.shape[0] // 4
    return jnp.concatenate([x[:h], x[2 * h : 3 * h], x[h : 2 * h], x[3 * h :]], 0)


def gather_adjoints(x):
    h = x.shape[0] // 2
    beside = send(x, DP, 0, 1)
    before, after = send(x, "x", 1), send(x, "x", 3)
    before_beside, after_beside = send(x, DP, 1, 1), send(x, DP, 3, 1)
    up = send(jnp.concatenate([before[:h], before_beside[:h]], 0), "x", 1)
    down = send(jnp.concatenate([after[h:], after_beside[h:]], 0), "x", 3)
    groups = ((x, beside), (after, after_beside), (before, before_beside, up, down))
    return [jnp.concatenate(group, 0) for group in groups]


def shards(c_guess, adj_guess, norm_gain, w_up, w_down, coarse_rate):
    position = lax.axis_index(LAYER)
    leading = position == 0
    trailing = position == lax.axis_size(LAYER) - 1
    part = lax.axis_index(DP).astype(jnp.int32)[None]
    start = c_guess[0]
    guess = adj_guess[0]
    decay = coarse_rate[0]
    rate = decay[None]
    w_up = pltpu.with_memory_space_constraint(w_up, pltpu.HBM)
    w_down = pltpu.with_memory_space_constraint(w_down, pltpu.HBM)

    shift = call_relax_forward(start, norm_gain, jnp.where(leading, 0.0, rate), w_up, w_down)
    carried, rates = forward_sweep(decay, shift)
    point = jnp.where(leading, start, carried)
    rounded = point.astype(bf16)
    beside = send(rounded, DP, 0, 1)
    shift, up_near, down_near = call_relax_adjoint(
        point, guess, norm_gain, jnp.where(trailing, 0.0, rate), w_up, w_down
    )
    shift, beside = lax.optimization_barrier((shift, beside))
    both = jnp.concatenate([rounded, beside], 0)

    def forward_of(points):
        return call_forward_parts(part, points, norm_gain, up_near, down_near)

    def beside_line(sent):
        sent, mine = lax.optimization_barrier((sent, both))
        others = [send(mine, "x", k) for k in (1, 3, 2)]
        return sent, (forward_of(mine), others)

    def beside_rows(sent, kept):
        parts, others = kept
        sent, parts = lax.optimization_barrier((sent, parts))
        rest = jnp.concatenate([others[0], far_order(others[2])], 0)
        return sent, (parts, rest, forward_of(others[1]))

    carried, (parts_own, rest, parts_after) = backward_sweep(
        rates, shift, beside_line, beside_rows
    )
    adjoint = jnp.where(trailing, guess, carried)
    rounded, rest = lax.optimization_barrier((adjoint.astype(bf16), rest))
    steps = zip(gather_adjoints(rounded), (parts_own, parts_after, forward_of(rest)))
    sums = None
    for adj, parts in steps:
        sums = call_backward_parts(adj, norm_gain, parts, up_near, down_near, sums)
    up_grad, down_grad = sums
    return (point[None], adjoint[None], up_grad, down_grad)


def solution(mesh):
    finer = Mesh(mesh.devices.reshape(4, 4, 2, 4, 2), LAYER + DP)
    placed = (
        P(LAYER, DP, None),
        P(LAYER, DP, None),
        P(LAYER, None),
        P(LAYER, None, None),
        P(LAYER, None, None),
        P(LAYER, None),
    )
    outs = (P(LAYER, DP, None),) * 4
    return jax.shard_map(shards, mesh=finer, in_specs=placed, out_specs=outs, check_vma=False)
```

```python
import jax
import jax.numpy as jnp
from jax import lax
from jax.experimental import pallas as pl
from jax.experimental.pallas import tpu as pltpu
from jax.sharding import Mesh
from jax.sharding import PartitionSpec as P

LAYER = ("y", "zh", "c")
DP = ("x", "zl")

eps = 1e-06
step_length = 0.5
f32 = jnp.float32
bf16 = jnp.bfloat16
CHUNK = 512
UNROLL = 2
BLOCK = 256
VMEM = pl.BlockSpec(memory_space=pltpu.VMEM)
ANY = pl.BlockSpec(memory_space=pl.ANY)
SMEM = pl.BlockSpec(memory_space=pltpu.SMEM)


def dot(a, b):
    return jnp.dot(a, b, preferred_element_type=f32)


def dot_t(a, b):
    return lax.dot_general(a, b, (((1,), (1,)), ((), ())), preferred_element_type=f32)


def dot_tokens(a, b):
    return lax.dot_general(a, b, (((0,), (0,)), ((), ())), preferred_element_type=f32)


def normalize(state):
    inverse_rms = lax.rsqrt(jnp.mean(state * state, axis=-1, keepdims=True) + eps)
    return state * inverse_rms, inverse_rms


def silu_parts(preact):
    s = 0.5 + 0.5 * jnp.tanh(0.5 * preact)
    hidden = preact * s
    return hidden, s + (hidden - hidden * s)


def input_cotangent(cotangent, normed_grad, unit, inverse_rms, gain):
    unit_grad = normed_grad * gain
    inner = jnp.mean(unit_grad * unit, axis=-1, keepdims=True)
    return cotangent + inverse_rms * (unit_grad - unit * inner)


def weight_copies(up_hbm, down_hbm, up, down, sems, wanted):
    copies = {}
    for n, (kind, layer) in enumerate(wanted):
        src, dst = (up_hbm, up) if kind == "up" else (down_hbm, down)
        copies[kind, layer] = pltpu.make_async_copy(src.at[layer], dst.at[layer], sems.at[n])
    return copies


def chunks(width):
    return [slice(n, n + CHUNK) for n in range(0, width, CHUNK)]


def relax_forward(
    keep, start_hbm, gain_hbm, rate_hbm, up_hbm, down_hbm,
    shift, start, gain, rate, up, down, hidden, sems, small_sems,
):
    small = [
        pltpu.make_async_copy(start_hbm.at[0], start, small_sems.at[0]),
        pltpu.make_async_copy(gain_hbm, gain, small_sems.at[1]),
        pltpu.make_async_copy(rate_hbm, rate, small_sems.at[2]),
    ]
    wanted = [("up", 0), ("down", 0), ("up", 1), ("down", 1)]
    copies = weight_copies(up_hbm, down_hbm, up, down, sems, wanted)
    for copy in (*small, *copies.values()):
        copy.start()
    for copy in small:
        copy.wait()
    state = start[...]
    for layer in (0, 1):
        unit, _ = normalize(state)
        normed = (unit * gain[layer : layer + 1]).astype(bf16)
        copies["up", layer].wait()
        for cols in chunks(hidden.shape[1]):
            h, _ = silu_parts(dot(normed, up[layer, :, cols]))
            hidden[:, cols] = h.astype(bf16)
        copies["down", layer].wait()
        state = state + step_length * dot(hidden[...], down[layer])
    shift[...] = state - keep[0] * (rate[...] * start[...])


def prepare(guess, up_hbm, down_hbm, hidden_grad, up, down, sems):
    wanted = [("down", 1), ("up", 0), ("down", 0), ("up", 1)]
    copies = weight_copies(up_hbm, down_hbm, up, down, sems, wanted)
    for copy in copies.values():
        copy.start()
    out_grad = (step_length * guess[...]).astype(bf16)
    copies["down", 1].wait()
    for cols in chunks(hidden_grad.shape[1]):
        hidden_grad[:, cols] = dot_t(out_grad, down[1, cols, :])
    for key in wanted[1:]:
        copies[key].wait()


def relax_adjoint(
    point, guess, gain, rate, hidden_grad, up, down, shift, hidden, slope, pre_grad
):
    ff = chunks(hidden.shape[1])
    g0, g1 = gain[0:1], gain[1:2]
    unit0, inv0 = normalize(point[...])
    normed = (unit0 * g0).astype(bf16)
    for cols in ff:
        h, sl = silu_parts(dot(normed, up[0, :, cols]))
        hidden[:, cols] = h.astype(bf16)
        slope[:, cols] = sl
    state = point[...] + step_length * dot(hidden[...], down[0])
    unit1, inv1 = normalize(state)
    normed = (unit1 * g1).astype(bf16)
    for cols in ff:
        _, sl = silu_parts(dot(normed, up[1, :, cols]))
        pre_grad[:, cols] = (hidden_grad[:, cols] * sl).astype(bf16)
    cot = input_cotangent(guess[...], dot_t(pre_grad[...], up[1]), unit1, inv1, g1)
    out_grad = (step_length * cot).astype(bf16)
    for cols in ff:
        pre_grad[:, cols] = (dot_t(out_grad, down[0, cols, :]) * slope[:, cols]).astype(bf16)
    begin = input_cotangent(cot, dot_t(pre_grad[...], up[0]), unit0, inv0, g0)
    shift[...] = begin - rate[...] * guess[...]


def forward_parts(
    part, points, gain, up, down,
    slope0, slope1, state1, normed0, normed1, hidden0, hidden1,
    hidden,
):
    me = part[0]
    steps = hidden.shape[1] // CHUNK
    width = gain.shape[1]
    ff_own = pl.ds(pl.multiple_of(me * 256, 256), 256)
    rows = lax.broadcasted_iota(jnp.int32, (normed0.shape[0], width), 0)
    cols_of = lax.broadcasted_iota(jnp.int32, (normed0.shape[0], width), 1)
    pick = jnp.where(cols_of == rows + me * normed0.shape[0], 1.0, 0.0).astype(bf16)
    point = points[...].astype(f32)
    unit, _ = normalize(point)
    normed = (unit * gain[0:1]).astype(bf16)
    normed0[...] = dot_t(pick, normed).astype(bf16)
    @pl.loop(0, steps // UNROLL)
    def _(n):
        for k in range(UNROLL):
            cols = pl.ds(pl.multiple_of((n * UNROLL + k) * CHUNK, CHUNK), CHUNK)
            h, sl = silu_parts(dot(normed, up[0, :, cols]))
            hidden[:, cols] = h.astype(bf16)
            slope0[:, cols] = sl.astype(bf16)

    hidden0[...] = hidden[:, ff_own]
    state = point + step_length * dot(hidden[...], down[0])
    state1[...] = state.astype(bf16)
    unit, _ = normalize(state)
    normed = (unit * gain[1:2]).astype(bf16)
    normed1[...] = dot_t(pick, normed).astype(bf16)
    @pl.loop(0, steps // UNROLL)
    def _(n):
        for k in range(UNROLL):
            cols = pl.ds(pl.multiple_of((n * UNROLL + k) * CHUNK, CHUNK), CHUNK)
            h, sl = silu_parts(dot(normed, up[1, :, cols]))
            hidden[:, cols] = h.astype(bf16)
            slope1[:, cols] = sl.astype(bf16)

    hidden1[...] = hidden[:, ff_own]


def backward_parts(
    adj, gain, slope0, slope1, state1, normed0, normed1, hidden0, hidden1,
    up, down, up_old, down_old,
    up_grad, down_grad, pre_grad,
):
    first = pl.program_id(0) == 0

    @pl.when(first)
    def _():
        if up_old is None:
            up_grad[...] = jnp.zeros_like(up_grad)
            down_grad[...] = jnp.zeros_like(down_grad)
        else:
            up_grad[...] = up_old[...]
            down_grad[...] = down_old[...]

    steps = pre_grad.shape[1] // CHUNK
    cot = adj[...].astype(f32)
    out_grad = (step_length * cot).astype(bf16)
    @pl.loop(0, steps // UNROLL)
    def _(n):
        for k in range(UNROLL):
            cols = pl.ds(pl.multiple_of((n * UNROLL + k) * CHUNK, CHUNK), CHUNK)
            pg = (dot_t(out_grad, down[1, cols, :]) * slope1[:, cols].astype(f32)).astype(bf16)
            pre_grad[:, cols] = pg
            up_grad[1, :, cols] += dot(normed1[...], pg)

    down_grad[1] += dot_tokens(hidden1[...], out_grad)
    unit, inv = normalize(state1[...].astype(f32))
    cot = input_cotangent(cot, dot_t(pre_grad[...], up[1]), unit, inv, gain[1:2])
    out_grad = (step_length * cot).astype(bf16)
    @pl.loop(0, steps // UNROLL)
    def _(n):
        for k in range(UNROLL):
            cols = pl.ds(pl.multiple_of((n * UNROLL + k) * CHUNK, CHUNK), CHUNK)
            pg = (dot_t(out_grad, down[0, cols, :]) * slope0[:, cols].astype(f32)).astype(bf16)
            up_grad[0, :, cols] += dot(normed0[...], pg)

    down_grad[0] += dot_tokens(hidden0[...], out_grad)


def backward_parts_first(adj, gain, s0, s1, st, n0, n1, h0, h1, uh, dh, *rest):
    backward_parts(adj, gain, s0, s1, st, n0, n1, h0, h1, uh, dh, None, None, *rest)


def shape(dims, dtype):
    return jax.ShapeDtypeStruct(dims, dtype)


def cost(tokens, matmuls):
    flops = int(2 * tokens * 512 * 2048 * matmuls)
    return pl.CostEstimate(flops=flops, bytes_accessed=8 << 20, transcendentals=0)


def weight_scratch(up, down, n):
    return [pltpu.VMEM(up.shape, bf16), pltpu.VMEM(down.shape, bf16)], [pltpu.SemaphoreType.DMA((n,))]


def call_relax_forward(keep, start, gain, rate, up, down):
    _, tokens, width = start.shape
    ff = up.shape[2]
    weights, sems = weight_scratch(up, down, 4)
    return pl.pallas_call(
        relax_forward,
        out_shape=shape((tokens, width), f32),
        in_specs=[SMEM, ANY, ANY, ANY, ANY, ANY],
        out_specs=VMEM,
        scratch_shapes=[
            pltpu.VMEM((tokens, width), f32), pltpu.VMEM(gain.shape, f32), pltpu.VMEM(rate.shape, f32),
            *weights, pltpu.VMEM((tokens, ff), bf16), *sems, pltpu.SemaphoreType.DMA((3,)),
        ],
        compiler_params=pltpu.CompilerParams(vmem_limit_bytes=24 << 20),
        cost_estimate=cost(tokens, 4),
        name="relax_forward",
    )(keep, *(pltpu.with_memory_space_constraint(a, pltpu.HBM) for a in (start, gain, rate)), up, down)


def call_prepare(guess, up, down):
    tokens = guess.shape[0]
    return pl.pallas_call(
        prepare,
        out_shape=(
            shape((tokens, up.shape[2]), f32), pltpu.VMEM(up.shape, bf16), pltpu.VMEM(down.shape, bf16),
        ),
        in_specs=[VMEM, ANY, ANY],
        out_specs=(VMEM, VMEM, VMEM),
        scratch_shapes=[pltpu.SemaphoreType.DMA((4,))],
        compiler_params=pltpu.CompilerParams(vmem_limit_bytes=16 << 20),
        cost_estimate=cost(tokens, 2),
        name="prepare",
    )(guess, up, down)


def call_relax_adjoint(point, guess, gain, rate, hidden_grad, up, down):
    tokens, width = point.shape
    ff = up.shape[2]
    return pl.pallas_call(
        relax_adjoint,
        out_shape=shape((tokens, width), f32),
        in_specs=[VMEM] * 7,
        out_specs=VMEM,
        scratch_shapes=[
            pltpu.VMEM((tokens, ff), bf16),
            pltpu.VMEM((tokens, ff), f32),
            pltpu.VMEM((tokens, ff), bf16),
        ],
        compiler_params=pltpu.CompilerParams(
            vmem_limit_bytes=16 << 20
        ),
        cost_estimate=cost(tokens, 6),
        name="relax_adjoint",
    )(point, guess, gain, rate, hidden_grad, up, down)


def by_rows(width):
    return pl.BlockSpec((BLOCK, width), lambda i: (i, 0))


def by_cols(rows):
    return pl.BlockSpec((rows, BLOCK), lambda i: (0, i))


def whole(dims):
    return pl.BlockSpec(dims, lambda i: (0,) * len(dims))


def call_forward_parts(part, points, gain, up, down):
    tokens, width = points.shape
    ff = up.shape[2]
    own = ff // 8
    return pl.pallas_call(
        forward_parts,
        grid=(tokens // BLOCK,),
        out_shape=(
            shape((tokens, ff), bf16), shape((tokens, ff), bf16), shape((tokens, width), bf16),
            shape((width // 8, tokens), bf16), shape((width // 8, tokens), bf16),
            shape((tokens, own), bf16), shape((tokens, own), bf16),
        ),
        in_specs=[SMEM, by_rows(width), whole(gain.shape), VMEM, VMEM],
        out_specs=(
            by_rows(ff), by_rows(ff), by_rows(width), by_cols(width // 8), by_cols(width // 8),
            by_rows(own), by_rows(own),
        ),
        scratch_shapes=[pltpu.VMEM((BLOCK, ff), bf16)],
        compiler_params=pltpu.CompilerParams(
            vmem_limit_bytes=24 << 20, dimension_semantics=("arbitrary",)
        ),
        cost_estimate=cost(tokens, 3),
        name="forward_parts",
    )(part, points, gain, up, down)


def call_backward_parts(adj, gain, parts, up, down, old=None):
    tokens, width = adj.shape
    ff = up.shape[2]
    own = ff // 8
    up_dims, down_dims = (2, width // 8, ff), (2, own, width)
    more = [] if old is None else [whole(up_dims), whole(down_dims)]
    return pl.pallas_call(
        backward_parts_first if old is None else backward_parts,
        grid=(tokens // BLOCK,),
        out_shape=(shape(up_dims, f32), shape(down_dims, f32)),
        in_specs=[
            by_rows(width), whole(gain.shape), by_rows(ff), by_rows(ff), by_rows(width),
            by_cols(width // 8), by_cols(width // 8), by_rows(own), by_rows(own), VMEM, VMEM, *more,
        ],
        out_specs=(whole(up_dims), whole(down_dims)),
        scratch_shapes=[pltpu.VMEM((BLOCK, ff), bf16)],
        compiler_params=pltpu.CompilerParams(
            vmem_limit_bytes=24 << 20, dimension_semantics=("arbitrary",)
        ),
        cost_estimate=cost(tokens, 3.5),
        name="backward_parts",
    )(adj, gain, *parts, up, down, *(old or ()))


def shift_pairs(size, k):
    return [(i, (i + k) % size) for i in range(size)]


def split_rows(a):
    hi = a.astype(bf16)
    lo = (a - hi.astype(f32)).astype(bf16)
    return hi, lo


def exchange_cores(x):
    return lax.ppermute(x, "c", [(0, 1), (1, 0)])


def line_exchange(payload, axis):
    return [lax.ppermute(payload, axis, shift_pairs(4, k)) for k in (1, 2, 3)]


def pack(rate, shift):
    hi, lo = split_rows(rate)
    pad = jnp.zeros((14, rate.shape[-1]), bf16)
    return jnp.concatenate([shift.astype(bf16), hi, lo, pad], 0)


def unpack(payload, rows):
    shift = payload[:rows].astype(f32)
    rate = payload[rows : rows + 1].astype(f32) + payload[rows + 1 : rows + 2].astype(f32)
    return rate, shift


def fold(pieces, carry, rate, mask, order):
    for k in order:
        a, b = pieces[k - 1]
        keep = mask(k)
        carry = jnp.where(keep, a * carry + b, carry)
        rate = jnp.where(keep, a * rate, rate)
    return rate, carry


def forward_sweep(decay, shift, beside_rows):
    c = lax.axis_index("c")
    zh = lax.axis_index("zh")
    y = lax.axis_index("y")
    half = shift.shape[0] // 2
    first = c == 0
    width = shift.shape[1]
    low, high = shift[:half], shift[half:]
    mine = jnp.where(first, low, high)
    give = jnp.concatenate(
        [jnp.where(first, high, low), jnp.broadcast_to(decay[None], (8, width))], 0
    )
    got = exchange_cores(give)
    other, other_rate = got[:half], got[half : half + 1]
    rate0 = jnp.where(first, decay[None], other_rate)
    rate1 = jnp.where(first, other_rate, decay[None])
    b0 = jnp.where(first, mine, other)
    b1 = jnp.where(first, other, mine)
    pair = (rate0 * rate1, rate1 * b0 + b1)
    pieces_z = [unpack(p, half) for p in line_exchange(pack(*pair), "zh")]
    one = jnp.ones_like(rate0)
    zero = jnp.zeros_like(b0)
    before_rate, before = fold(pieces_z, zero, one, lambda k: zh >= k, (3, 2, 1))
    row = (pair[0] * before_rate, pair[0] * before + pair[1])
    row = fold(pieces_z, row[1], row[0], lambda k: zh < k, (3, 2, 1))
    sent, kept = beside_rows(pack(*row))
    got, ready = lax.optimization_barrier((line_exchange(sent, "y"), kept[0]))
    pieces_y = [unpack(p, half) for p in got]
    _, rows_before = fold(pieces_y, zero, one, lambda k: y >= k, (3, 2, 1))
    entry = before_rate * rows_before + before
    later = rate0 * entry + b0
    got = exchange_cores(jnp.where(first, later, entry))
    own = jnp.where(first, entry, later)
    point = jnp.concatenate([jnp.where(first, own, got), jnp.where(first, got, own)], 0)
    rates = (rate0, rate1, [p[0] for p in pieces_z], [p[0] for p in pieces_y])
    return point, rates, (ready, *kept[1:])


def backward_sweep(rates, shift, beside_line, beside_rows):
    rate0, rate1, rates_z, rates_y = rates
    c = lax.axis_index("c")
    zh = lax.axis_index("zh")
    y = lax.axis_index("y")
    half = shift.shape[0] // 2
    first = c == 0
    low, high = shift[:half], shift[half:]
    mine = jnp.where(first, low, high)
    other = exchange_cores(jnp.where(first, high, low))
    b0 = jnp.where(first, mine, other)
    b1 = jnp.where(first, other, mine)
    pair_rate, pair = rate0 * rate1, rate0 * b1 + b0
    sent, kept = beside_line(pair.astype(bf16))
    got = line_exchange(sent, "zh")
    pieces_z = [(a, p.astype(f32)) for a, p in zip(rates_z, got)]
    one = jnp.ones_like(rate0)
    zero = jnp.zeros_like(b0)
    after_rate, after = fold(pieces_z, zero, one, lambda k: zh < k, (1, 2, 3))
    _, row = fold(pieces_z, pair_rate * after + pair, one, lambda k: zh >= k, (1, 2, 3))
    sent, kept = beside_rows(row.astype(bf16), kept)
    got, finished = lax.optimization_barrier((line_exchange(sent, "y"), kept[2]))
    kept = (*kept[:2], finished)
    pieces_y = [(a, p.astype(f32)) for a, p in zip(rates_y, got)]
    _, rows_after = fold(pieces_y, zero, one, lambda k: y < k, (1, 2, 3))
    entry = after_rate * rows_after + after
    earlier = rate1 * entry + b1
    got = exchange_cores(jnp.where(first, entry, earlier))
    own = jnp.where(first, earlier, entry)
    carried = jnp.concatenate([jnp.where(first, own, got), jnp.where(first, got, own)], 0)
    return carried, kept


def send(x, axes, dx, dz=None):
    if dz is None:
        return lax.ppermute(x, "x", shift_pairs(4, dx))
    pairs = [(a * 2 + b, (a + dx) % 4 * 2 + (b + dz) % 2) for a in range(4) for b in range(2)]
    return lax.ppermute(x, DP, pairs)


def far_order(x):
    h = x.shape[0] // 4
    return jnp.concatenate([x[:h], x[2 * h : 3 * h], x[h : 2 * h], x[3 * h :]], 0)


def gather_adjoints(x):
    h = x.shape[0] // 2
    beside = send(x, DP, 0, 1)
    before, after = send(x, "x", 1), send(x, "x", 3)
    before_beside, after_beside = send(x, DP, 1, 1), send(x, DP, 3, 1)
    up = send(jnp.concatenate([before[:h], before_beside[:h]], 0), "x", 1)
    down = send(jnp.concatenate([after[h:], after_beside[h:]], 0), "x", 3)
    groups = ((x, beside), (after, after_beside), (before, before_beside, up, down))
    return [jnp.concatenate(group, 0) for group in groups]


def shards(c_guess, adj_guess, norm_gain, w_up, w_down, coarse_rate):
    position = lax.axis_index(LAYER)
    leading = position == 0
    trailing = position == lax.axis_size(LAYER) - 1
    part = lax.axis_index(DP).astype(jnp.int32)[None]
    start = c_guess[0]
    guess = adj_guess[0]
    decay = coarse_rate[0]
    rate = decay[None]
    w_up = pltpu.with_memory_space_constraint(w_up, pltpu.HBM)
    w_down = pltpu.with_memory_space_constraint(w_down, pltpu.HBM)

    def load_beside(sent):
        sent, cotangent = lax.optimization_barrier((sent, guess))
        return sent, call_prepare(cotangent, w_up, w_down)

    keep = jnp.where(leading, 0.0, 1.0)[None]
    shift = call_relax_forward(keep, c_guess, norm_gain, coarse_rate, w_up, w_down)
    carried, rates, loaded = forward_sweep(decay, shift, load_beside)
    hidden_grad, up_near, down_near = loaded
    point = jnp.where(leading, start, carried)
    rounded = point.astype(bf16)
    beside = send(rounded, DP, 0, 1)
    shift = call_relax_adjoint(
        point, guess, norm_gain, jnp.where(trailing, 0.0, rate), hidden_grad, up_near, down_near
    )
    shift, beside = lax.optimization_barrier((shift, beside))
    both = jnp.concatenate([rounded, beside], 0)

    def forward_of(points):
        return call_forward_parts(part, points, norm_gain, up_near, down_near)

    def beside_line(sent):
        sent, mine = lax.optimization_barrier((sent, both))
        others = [send(mine, "x", k) for k in (1, 3, 2)]
        return sent, (forward_of(mine), others)

    def beside_rows(sent, kept):
        parts, others = kept
        sent, parts = lax.optimization_barrier((sent, parts))
        rest = jnp.concatenate([others[0], far_order(others[2])], 0)
        return sent, (parts, rest, forward_of(others[1]))

    carried, (parts_own, rest, parts_after) = backward_sweep(
        rates, shift, beside_line, beside_rows
    )
    adjoint = jnp.where(trailing, guess, carried)
    rounded, rest = lax.optimization_barrier((adjoint.astype(bf16), rest))
    steps = zip(gather_adjoints(rounded), (parts_own, parts_after, forward_of(rest)))
    sums = None
    for adj, parts in steps:
        sums = call_backward_parts(adj, norm_gain, parts, up_near, down_near, sums)
    up_grad, down_grad = sums
    return (point[None], adjoint[None], up_grad, down_grad)


def solution(mesh):
    finer = Mesh(mesh.devices.reshape(4, 4, 2, 4, 2), LAYER + DP)
    placed = (
        P(LAYER, DP, None),
        P(LAYER, DP, None),
        P(LAYER, None),
        P(LAYER, None, None),
        P(LAYER, None, None),
        P(LAYER, None),
    )
    outs = (P(LAYER, DP, None),) * 4
    return jax.shard_map(shards, mesh=finer, in_specs=placed, out_specs=outs, check_vma=False)
```

```python
import functools

import jax
import jax.numpy as jnp
from jax import lax
from jax.experimental import pallas as pl
from jax.experimental.pallas import tpu as pltpu
from jax.sharding import Mesh
from jax.sharding import PartitionSpec as P

LAYER = ("y", "zh", "c")
DP = ("x", "zl")

eps = 1e-06
step_length = 0.5
f32 = jnp.float32
bf16 = jnp.bfloat16
CHUNK = 512
UNROLL = 2
BLOCK = 256
VMEM = pl.BlockSpec(memory_space=pltpu.VMEM)
ANY = pl.BlockSpec(memory_space=pl.ANY)
SMEM = pl.BlockSpec(memory_space=pltpu.SMEM)


def dot(a, b):
    return jnp.dot(a, b, preferred_element_type=f32)


def dot_t(a, b):
    return lax.dot_general(a, b, (((1,), (1,)), ((), ())), preferred_element_type=f32)


def dot_tokens(a, b):
    return lax.dot_general(a, b, (((0,), (0,)), ((), ())), preferred_element_type=f32)


def normalize(state):
    inverse_rms = lax.rsqrt(jnp.mean(state * state, axis=-1, keepdims=True) + eps)
    return state * inverse_rms, inverse_rms


def silu_parts(preact):
    s = 0.5 + 0.5 * jnp.tanh(0.5 * preact)
    hidden = preact * s
    return hidden, s + (hidden - hidden * s)


def input_cotangent(cotangent, normed_grad, unit, inverse_rms, gain):
    unit_grad = normed_grad * gain
    inner = jnp.mean(unit_grad * unit, axis=-1, keepdims=True)
    return cotangent + inverse_rms * (unit_grad - unit * inner)


def weight_copies(up_hbm, down_hbm, up, down, sems, wanted):
    copies = {}
    for n, (kind, layer) in enumerate(wanted):
        src, dst = (up_hbm, up) if kind == "up" else (down_hbm, down)
        copies[kind, layer] = pltpu.make_async_copy(src.at[layer], dst.at[layer], sems.at[n])
    return copies


def chunks(width):
    return [slice(n, n + CHUNK) for n in range(0, width, CHUNK)]


def relax_forward(
    keep, start_hbm, gain_hbm, rate_hbm, up_hbm, down_hbm,
    shift, start, gain, rate, up, down, hidden, sems, small_sems,
):
    small = [
        pltpu.make_async_copy(start_hbm.at[0], start, small_sems.at[0]),
        pltpu.make_async_copy(gain_hbm, gain, small_sems.at[1]),
        pltpu.make_async_copy(rate_hbm, rate, small_sems.at[2]),
    ]
    wanted = [("up", 0), ("down", 0), ("up", 1), ("down", 1)]
    copies = weight_copies(up_hbm, down_hbm, up, down, sems, wanted)
    for copy in (*small, *copies.values()):
        copy.start()
    for copy in small:
        copy.wait()
    state = start[...]
    for layer in (0, 1):
        unit, _ = normalize(state)
        normed = (unit * gain[layer : layer + 1]).astype(bf16)
        copies["up", layer].wait()
        for cols in chunks(hidden.shape[1]):
            h, _ = silu_parts(dot(normed, up[layer, :, cols]))
            hidden[:, cols] = h.astype(bf16)
        copies["down", layer].wait()
        state = state + step_length * dot(hidden[...], down[layer])
    shift[...] = state - keep[0] * (rate[...] * start[...])


def prepare(guess, up_hbm, down_hbm, hidden_grad, up, down, sems):
    wanted = [("down", 1), ("up", 0), ("down", 0), ("up", 1)]
    copies = weight_copies(up_hbm, down_hbm, up, down, sems, wanted)
    for copy in copies.values():
        copy.start()
    out_grad = (step_length * guess[...]).astype(bf16)
    copies["down", 1].wait()
    for cols in chunks(hidden_grad.shape[1]):
        hidden_grad[:, cols] = dot_t(out_grad, down[1, cols, :])
    for key in wanted[1:]:
        copies[key].wait()


def relax_adjoint(
    point, guess, gain, rate, hidden_grad, up, down, shift, hidden, slope, pre_grad
):
    ff = chunks(hidden.shape[1])
    g0, g1 = gain[0:1], gain[1:2]
    unit0, inv0 = normalize(point[...])
    normed = (unit0 * g0).astype(bf16)
    for cols in ff:
        h, sl = silu_parts(dot(normed, up[0, :, cols]))
        hidden[:, cols] = h.astype(bf16)
        slope[:, cols] = sl
    state = point[...] + step_length * dot(hidden[...], down[0])
    unit1, inv1 = normalize(state)
    normed = (unit1 * g1).astype(bf16)
    for cols in ff:
        _, sl = silu_parts(dot(normed, up[1, :, cols]))
        pre_grad[:, cols] = (hidden_grad[:, cols] * sl).astype(bf16)
    cot = input_cotangent(guess[...], dot_t(pre_grad[...], up[1]), unit1, inv1, g1)
    out_grad = (step_length * cot).astype(bf16)
    for cols in ff:
        pre_grad[:, cols] = (dot_t(out_grad, down[0, cols, :]) * slope[:, cols]).astype(bf16)
    begin = input_cotangent(cot, dot_t(pre_grad[...], up[0]), unit0, inv0, g0)
    shift[...] = begin - rate[...] * guess[...]


def forward_parts(
    part, points, gain, up, down,
    slope0, slope1, state1, normed0, normed1, hidden0, hidden1,
    hidden,
):
    me = part[0]
    steps = hidden.shape[1] // CHUNK
    width = gain.shape[1]
    ff_own = pl.ds(pl.multiple_of(me * 256, 256), 256)
    rows = lax.broadcasted_iota(jnp.int32, (normed0.shape[0], width), 0)
    cols_of = lax.broadcasted_iota(jnp.int32, (normed0.shape[0], width), 1)
    pick = jnp.where(cols_of == rows + me * normed0.shape[0], 1.0, 0.0).astype(bf16)
    point = points[...].astype(f32)
    unit, _ = normalize(point)
    normed = (unit * gain[0:1]).astype(bf16)
    normed0[...] = dot_t(pick, normed).astype(bf16)
    @pl.loop(0, steps // UNROLL)
    def _(n):
        for k in range(UNROLL):
            cols = pl.ds(pl.multiple_of((n * UNROLL + k) * CHUNK, CHUNK), CHUNK)
            h, sl = silu_parts(dot(normed, up[0, :, cols]))
            hidden[:, cols] = h.astype(bf16)
            slope0[:, cols] = sl.astype(bf16)

    hidden0[...] = hidden[:, ff_own]
    state = point + step_length * dot(hidden[...], down[0])
    state1[...] = state.astype(bf16)
    unit, _ = normalize(state)
    normed = (unit * gain[1:2]).astype(bf16)
    normed1[...] = dot_t(pick, normed).astype(bf16)
    @pl.loop(0, steps // UNROLL)
    def _(n):
        for k in range(UNROLL):
            cols = pl.ds(pl.multiple_of((n * UNROLL + k) * CHUNK, CHUNK), CHUNK)
            h, sl = silu_parts(dot(normed, up[1, :, cols]))
            hidden[:, cols] = h.astype(bf16)
            slope1[:, cols] = sl.astype(bf16)

    hidden1[...] = hidden[:, ff_own]


def backward_parts(
    single, adj, gain, slope0, slope1, state1, normed0, normed1, hidden0, hidden1,
    up, down, up_old, down_old,
    up_grad, down_grad, pre_grad,
):
    first = pl.program_id(0) == 0

    if not single:

        @pl.when(first)
        def _():
            up_grad[...] = up_old[...]
            down_grad[...] = down_old[...]

    def add(total, old, at, value):
        if not single:
            old = total
        total[at] = value if old is None else old[at] + value

    steps = pre_grad.shape[1] // CHUNK
    cot = adj[...].astype(f32)
    out_grad = (step_length * cot).astype(bf16)
    @pl.loop(0, steps // UNROLL)
    def _(n):
        for k in range(UNROLL):
            cols = pl.ds(pl.multiple_of((n * UNROLL + k) * CHUNK, CHUNK), CHUNK)
            pg = (dot_t(out_grad, down[1, cols, :]) * slope1[:, cols].astype(f32)).astype(bf16)
            pre_grad[:, cols] = pg
            add(up_grad, up_old, (1, slice(None), cols), dot(normed1[...], pg))

    add(down_grad, down_old, 1, dot_tokens(hidden1[...], out_grad))
    unit, inv = normalize(state1[...].astype(f32))
    cot = input_cotangent(cot, dot_t(pre_grad[...], up[1]), unit, inv, gain[1:2])
    out_grad = (step_length * cot).astype(bf16)
    @pl.loop(0, steps // UNROLL)
    def _(n):
        for k in range(UNROLL):
            cols = pl.ds(pl.multiple_of((n * UNROLL + k) * CHUNK, CHUNK), CHUNK)
            pg = (dot_t(out_grad, down[0, cols, :]) * slope0[:, cols].astype(f32)).astype(bf16)
            add(up_grad, up_old, (0, slice(None), cols), dot(normed0[...], pg))

    add(down_grad, down_old, 0, dot_tokens(hidden0[...], out_grad))


def backward_parts_first(single, adj, gain, s0, s1, st, n0, n1, h0, h1, uh, dh, *rest):
    backward_parts(single, adj, gain, s0, s1, st, n0, n1, h0, h1, uh, dh, None, None, *rest)


def shape(dims, dtype):
    return jax.ShapeDtypeStruct(dims, dtype)


def cost(tokens, matmuls):
    flops = int(2 * tokens * 512 * 2048 * matmuls)
    return pl.CostEstimate(flops=flops, bytes_accessed=8 << 20, transcendentals=0)


def weight_scratch(up, down, n):
    return [pltpu.VMEM(up.shape, bf16), pltpu.VMEM(down.shape, bf16)], [pltpu.SemaphoreType.DMA((n,))]


def call_relax_forward(keep, start, gain, rate, up, down):
    _, tokens, width = start.shape
    ff = up.shape[2]
    weights, sems = weight_scratch(up, down, 4)
    return pl.pallas_call(
        relax_forward,
        out_shape=shape((tokens, width), f32),
        in_specs=[SMEM, ANY, ANY, ANY, ANY, ANY],
        out_specs=VMEM,
        scratch_shapes=[
            pltpu.VMEM((tokens, width), f32), pltpu.VMEM(gain.shape, f32), pltpu.VMEM(rate.shape, f32),
            *weights, pltpu.VMEM((tokens, ff), bf16), *sems, pltpu.SemaphoreType.DMA((3,)),
        ],
        compiler_params=pltpu.CompilerParams(vmem_limit_bytes=24 << 20),
        cost_estimate=cost(tokens, 4),
        name="relax_forward",
    )(keep, *(pltpu.with_memory_space_constraint(a, pltpu.HBM) for a in (start, gain, rate)), up, down)


def call_prepare(guess, up, down):
    tokens = guess.shape[0]
    return pl.pallas_call(
        prepare,
        out_shape=(
            shape((tokens, up.shape[2]), f32), pltpu.VMEM(up.shape, bf16), pltpu.VMEM(down.shape, bf16),
        ),
        in_specs=[VMEM, ANY, ANY],
        out_specs=(VMEM, VMEM, VMEM),
        scratch_shapes=[pltpu.SemaphoreType.DMA((4,))],
        compiler_params=pltpu.CompilerParams(vmem_limit_bytes=16 << 20),
        cost_estimate=cost(tokens, 2),
        name="prepare",
    )(guess, up, down)


def call_relax_adjoint(point, guess, gain, rate, hidden_grad, up, down):
    tokens, width = point.shape
    ff = up.shape[2]
    return pl.pallas_call(
        relax_adjoint,
        out_shape=shape((tokens, width), f32),
        in_specs=[VMEM] * 7,
        out_specs=VMEM,
        scratch_shapes=[
            pltpu.VMEM((tokens, ff), bf16),
            pltpu.VMEM((tokens, ff), f32),
            pltpu.VMEM((tokens, ff), bf16),
        ],
        compiler_params=pltpu.CompilerParams(
            vmem_limit_bytes=16 << 20
        ),
        cost_estimate=cost(tokens, 6),
        name="relax_adjoint",
    )(point, guess, gain, rate, hidden_grad, up, down)


def by_rows(width):
    return pl.BlockSpec((BLOCK, width), lambda i: (i, 0))


def by_cols(rows):
    return pl.BlockSpec((rows, BLOCK), lambda i: (0, i))


def whole(dims):
    return pl.BlockSpec(dims, lambda i: (0,) * len(dims))


def call_forward_parts(part, points, gain, up, down):
    tokens, width = points.shape
    ff = up.shape[2]
    own = ff // 8
    return pl.pallas_call(
        forward_parts,
        grid=(tokens // BLOCK,),
        out_shape=(
            shape((tokens, ff), bf16), shape((tokens, ff), bf16), shape((tokens, width), bf16),
            shape((width // 8, tokens), bf16), shape((width // 8, tokens), bf16),
            shape((tokens, own), bf16), shape((tokens, own), bf16),
        ),
        in_specs=[SMEM, by_rows(width), whole(gain.shape), VMEM, VMEM],
        out_specs=(
            by_rows(ff), by_rows(ff), by_rows(width), by_cols(width // 8), by_cols(width // 8),
            by_rows(own), by_rows(own),
        ),
        scratch_shapes=[pltpu.VMEM((BLOCK, ff), bf16)],
        compiler_params=pltpu.CompilerParams(
            vmem_limit_bytes=24 << 20, dimension_semantics=("arbitrary",)
        ),
        cost_estimate=cost(tokens, 3),
        name="forward_parts",
    )(part, points, gain, up, down)


def call_backward_parts(adj, gain, parts, up, down, old=None):
    tokens, width = adj.shape
    ff = up.shape[2]
    own = ff // 8
    up_dims, down_dims = (2, width // 8, ff), (2, own, width)
    more = [] if old is None else [whole(up_dims), whole(down_dims)]
    return pl.pallas_call(
        functools.partial(
            backward_parts_first if old is None else backward_parts, tokens == BLOCK
        ),
        grid=(tokens // BLOCK,),
        out_shape=(shape(up_dims, f32), shape(down_dims, f32)),
        in_specs=[
            by_rows(width), whole(gain.shape), by_rows(ff), by_rows(ff), by_rows(width),
            by_cols(width // 8), by_cols(width // 8), by_rows(own), by_rows(own), VMEM, VMEM, *more,
        ],
        out_specs=(whole(up_dims), whole(down_dims)),
        scratch_shapes=[pltpu.VMEM((BLOCK, ff), bf16)],
        compiler_params=pltpu.CompilerParams(
            vmem_limit_bytes=24 << 20, dimension_semantics=("arbitrary",)
        ),
        cost_estimate=cost(tokens, 3.5),
        name="backward_parts",
    )(adj, gain, *parts, up, down, *(old or ()))


def shift_pairs(size, k):
    return [(i, (i + k) % size) for i in range(size)]


def split_rows(a):
    hi = a.astype(bf16)
    lo = (a - hi.astype(f32)).astype(bf16)
    return hi, lo


def exchange_cores(x):
    return lax.ppermute(x, "c", [(0, 1), (1, 0)])


def line_exchange(payload, axis):
    return [lax.ppermute(payload, axis, shift_pairs(4, k)) for k in (1, 2, 3)]


def pack(rate, shift):
    hi, lo = split_rows(rate)
    pad = jnp.zeros((14, rate.shape[-1]), bf16)
    return jnp.concatenate([shift.astype(bf16), hi, lo, pad], 0)


def unpack(payload, rows):
    shift = payload[:rows].astype(f32)
    rate = payload[rows : rows + 1].astype(f32) + payload[rows + 1 : rows + 2].astype(f32)
    return rate, shift


def fold(pieces, carry, rate, mask, order):
    for k in order:
        a, b = pieces[k - 1]
        keep = mask(k)
        carry = jnp.where(keep, a * carry + b, carry)
        rate = jnp.where(keep, a * rate, rate)
    return rate, carry


def forward_sweep(decay, shift, beside_rows):
    c = lax.axis_index("c")
    zh = lax.axis_index("zh")
    y = lax.axis_index("y")
    half = shift.shape[0] // 2
    first = c == 0
    width = shift.shape[1]
    low, high = shift[:half], shift[half:]
    mine = jnp.where(first, low, high)
    give = jnp.concatenate(
        [jnp.where(first, high, low), jnp.broadcast_to(decay[None], (8, width))], 0
    )
    got = exchange_cores(give)
    other, other_rate = got[:half], got[half : half + 1]
    rate0 = jnp.where(first, decay[None], other_rate)
    rate1 = jnp.where(first, other_rate, decay[None])
    b0 = jnp.where(first, mine, other)
    b1 = jnp.where(first, other, mine)
    pair = (rate0 * rate1, rate1 * b0 + b1)
    pieces_z = [unpack(p, half) for p in line_exchange(pack(*pair), "zh")]
    one = jnp.ones_like(rate0)
    zero = jnp.zeros_like(b0)
    before_rate, before = fold(pieces_z, zero, one, lambda k: zh >= k, (3, 2, 1))
    row = (pair[0] * before_rate, pair[0] * before + pair[1])
    row = fold(pieces_z, row[1], row[0], lambda k: zh < k, (3, 2, 1))
    sent, kept = beside_rows(pack(*row))
    got, ready = lax.optimization_barrier((line_exchange(sent, "y"), kept[0]))
    pieces_y = [unpack(p, half) for p in got]
    _, rows_before = fold(pieces_y, zero, one, lambda k: y >= k, (3, 2, 1))
    entry = before_rate * rows_before + before
    later = rate0 * entry + b0
    got = exchange_cores(jnp.where(first, later, entry))
    own = jnp.where(first, entry, later)
    point = jnp.concatenate([jnp.where(first, own, got), jnp.where(first, got, own)], 0)
    rates = (rate0, rate1, [p[0] for p in pieces_z], [p[0] for p in pieces_y])
    return point, rates, (ready, *kept[1:])


def backward_sweep(rates, shift, beside_line, beside_rows):
    rate0, rate1, rates_z, rates_y = rates
    c = lax.axis_index("c")
    zh = lax.axis_index("zh")
    y = lax.axis_index("y")
    half = shift.shape[0] // 2
    first = c == 0
    low, high = shift[:half], shift[half:]
    mine = jnp.where(first, low, high)
    other = exchange_cores(jnp.where(first, high, low))
    b0 = jnp.where(first, mine, other)
    b1 = jnp.where(first, other, mine)
    pair_rate, pair = rate0 * rate1, rate0 * b1 + b0
    sent, kept = beside_line(pair.astype(bf16))
    got = line_exchange(sent, "zh")
    pieces_z = [(a, p.astype(f32)) for a, p in zip(rates_z, got)]
    one = jnp.ones_like(rate0)
    zero = jnp.zeros_like(b0)
    after_rate, after = fold(pieces_z, zero, one, lambda k: zh < k, (1, 2, 3))
    _, row = fold(pieces_z, pair_rate * after + pair, one, lambda k: zh >= k, (1, 2, 3))
    sent, kept = beside_rows(row.astype(bf16), kept)
    got, finished = lax.optimization_barrier((line_exchange(sent, "y"), kept[2]))
    kept = (*kept[:2], finished)
    pieces_y = [(a, p.astype(f32)) for a, p in zip(rates_y, got)]
    _, rows_after = fold(pieces_y, zero, one, lambda k: y < k, (1, 2, 3))
    entry = after_rate * rows_after + after
    earlier = rate1 * entry + b1
    got = exchange_cores(jnp.where(first, entry, earlier))
    own = jnp.where(first, earlier, entry)
    carried = jnp.concatenate([jnp.where(first, own, got), jnp.where(first, got, own)], 0)
    return carried, kept


def send(x, axes, dx, dz=None):
    if dz is None:
        return lax.ppermute(x, "x", shift_pairs(4, dx))
    pairs = [(a * 2 + b, (a + dx) % 4 * 2 + (b + dz) % 2) for a in range(4) for b in range(2)]
    return lax.ppermute(x, DP, pairs)


def far_order(x):
    h = x.shape[0] // 4
    return jnp.concatenate([x[:h], x[2 * h : 3 * h], x[h : 2 * h], x[3 * h :]], 0)


def gather_adjoints(x):
    h = x.shape[0] // 2
    beside = send(x, DP, 0, 1)
    before, after = send(x, "x", 1), send(x, "x", 3)
    before_beside, after_beside = send(x, DP, 1, 1), send(x, DP, 3, 1)
    up = send(jnp.concatenate([before[:h], before_beside[:h]], 0), "x", 1)
    down = send(jnp.concatenate([after[h:], after_beside[h:]], 0), "x", 3)
    groups = ((x, beside), (after, after_beside), (before, before_beside, up, down))
    return [jnp.concatenate(group, 0) for group in groups]


def shards(c_guess, adj_guess, norm_gain, w_up, w_down, coarse_rate):
    position = lax.axis_index(LAYER)
    leading = position == 0
    trailing = position == lax.axis_size(LAYER) - 1
    part = lax.axis_index(DP).astype(jnp.int32)[None]
    start = c_guess[0]
    guess = adj_guess[0]
    decay = coarse_rate[0]
    rate = decay[None]
    w_up = pltpu.with_memory_space_constraint(w_up, pltpu.HBM)
    w_down = pltpu.with_memory_space_constraint(w_down, pltpu.HBM)

    def load_beside(sent):
        sent, cotangent = lax.optimization_barrier((sent, guess))
        return sent, call_prepare(cotangent, w_up, w_down)

    keep = jnp.where(leading, 0.0, 1.0)[None]
    shift = call_relax_forward(keep, c_guess, norm_gain, coarse_rate, w_up, w_down)
    carried, rates, loaded = forward_sweep(decay, shift, load_beside)
    hidden_grad, up_near, down_near = loaded
    point = jnp.where(leading, start, carried)
    rounded = point.astype(bf16)
    beside = send(rounded, DP, 0, 1)
    shift = call_relax_adjoint(
        point, guess, norm_gain, jnp.where(trailing, 0.0, rate), hidden_grad, up_near, down_near
    )
    shift, beside = lax.optimization_barrier((shift, beside))
    both = jnp.concatenate([rounded, beside], 0)

    def forward_of(points):
        return call_forward_parts(part, points, norm_gain, up_near, down_near)

    def beside_line(sent):
        sent, mine = lax.optimization_barrier((sent, both))
        others = [send(mine, "x", k) for k in (1, 3, 2)]
        return sent, (forward_of(mine), others)

    def beside_rows(sent, kept):
        parts, others = kept
        sent, parts = lax.optimization_barrier((sent, parts))
        rest = jnp.concatenate([others[0], far_order(others[2])], 0)
        return sent, (parts, rest, forward_of(others[1]))

    carried, (parts_own, rest, parts_after) = backward_sweep(
        rates, shift, beside_line, beside_rows
    )
    adjoint = jnp.where(trailing, guess, carried)
    rounded, rest = lax.optimization_barrier((adjoint.astype(bf16), rest))
    steps = zip(gather_adjoints(rounded), (parts_own, parts_after, forward_of(rest)))
    sums = None
    for adj, parts in steps:
        sums = call_backward_parts(adj, norm_gain, parts, up_near, down_near, sums)
    up_grad, down_grad = sums
    return (point[None], adjoint[None], up_grad, down_grad)


def solution(mesh):
    finer = Mesh(mesh.devices.reshape(4, 4, 2, 4, 2), LAYER + DP)
    placed = (
        P(LAYER, DP, None),
        P(LAYER, DP, None),
        P(LAYER, None),
        P(LAYER, None, None),
        P(LAYER, None, None),
        P(LAYER, None),
    )
    outs = (P(LAYER, DP, None),) * 4
    return jax.shard_map(shards, mesh=finer, in_specs=placed, out_specs=outs, check_vma=False)
```
